32 devices in a mesh: groups: 2 (over x), cols: 16 (over z, y, core).
Axes of the slice: x: 2, y: 2, z: 4, core: 2. Of those that a mesh axis runs over, the one named last changes fastest.
Arguments:
- left_feat: bfloat16 [4, 64, 256, 256], P('groups', None, 'cols'), parts along dimension 0, may hold values from -6 to 6
- right_feat: bfloat16 [4, 64, 256, 256], P('groups', None, 'cols'), parts along dimension 0, may hold values from -6 to 6
- bounds: int32 [4], P('groups'), parts along dimension 0, may hold values from 16 to 64, as said below
- disparity: int32 [4, 64, 256], P('groups', None, 'cols'), parts along dimension 0, may hold values from 0 to 63, as said below
- hidden_fine: bfloat16 [4, 64, 256, 128], P('groups', None, 'cols'), parts along dimension 0, may hold values from -1 to 1
- hidden_coarse: bfloat16 [4, 8, 32, 128], P('groups', None, 'cols'), parts along dimension 0, may hold values from -1 to 1
- motion_weight: bfloat16 [36, 128], replicated, may hold values from -1 to 1
- fine_gates: bfloat16 [9, 384, 256], replicated, may hold values from -0.109375 to 0.109375
- fine_candidate: bfloat16 [9, 384, 128], replicated, may hold values from -0.109375 to 0.109375
- coarse_gates: bfloat16 [9, 256, 256], replicated, may hold values from -0.125 to 0.125
- coarse_candidate: bfloat16 [9, 256, 128], replicated, may hold values from -0.125 to 0.125
Outputs:
- hidden_fine_new: bfloat16 [4, 64, 256, 128], P('groups', None, 'cols'), parts along dimension 0
- hidden_coarse_new: bfloat16 [4, 8, 32, 128], P('groups', None, 'cols'), parts along dimension 0
The draws below stay inside these ranges and needn't reach their ends.
There are 2 independent parts, one for each index of `groups`. The reference program is written for one: setup_inputs(seed, part) draws one part's arguments, and reference() takes and returns one part's arrays. A program takes and returns all parts, laid end to end along the dimension named above; an argument that names none is the same for every part. Nothing has to cross between parts.
Inputs may be any that keep to these rules, and one draw needn't show every extreme that they name: bounds[i] bounds the disparities of image pair i; in every draw one image pair has exactly 64. `disparity`: every entry lies below its image pair's bound; in every draw some entry equals 63.
All inputs are finite; a program needn't handle non-finite values.
Results may differ from the reference program's by a relative error of at most 0.0043.
Values may be sent and summed in bfloat16 or wider, within the bound.
No kernel may reach another device: no remote copies, remote signals or barrier semaphores. Data moves between devices by JAX's collectives and lax.ppermute only.
A program may use at most 64 MiB of HBM per device.

```python
import jax
import jax.numpy as jnp
from jax import lax

FEAT = 256
HID = 128
LEVELS = 4
RADIUS = 4
MAXD = 64
ROWS = 64
IMGS = 2
WIDTH = 256
CORR_CH = 36


def bound_draw(key):
    folded = jax.random.fold_in(key, 11)
    pick_key, spread_key = jax.random.split(folded)
    chosen = jax.random.randint(pick_key, (), 0, IMGS)
    others = jax.random.randint(spread_key, (IMGS,), MAXD // 4, MAXD + 1)
    limits = jnp.where(jnp.arange(IMGS) == chosen, MAXD, others).astype(jnp.int32)
    return (limits, chosen)


def draw_bounds(key, part):
    return bound_draw(key)[0]


def draw_disparity(key, part):
    limits, chosen = bound_draw(key)
    folded = jax.random.fold_in(key, 23)
    value_key, cell_key = jax.random.split(folded)
    values = jax.random.randint(value_key, (IMGS, ROWS, WIDTH), 0, limits[:, None, None])
    marked_cell = jax.random.randint(cell_key, (), 0, ROWS * WIDTH)
    flat_index = jnp.arange(ROWS * WIDTH).reshape(ROWS, WIDTH)
    marked = (jnp.arange(IMGS)[:, None, None] == chosen) & (flat_index[None] == marked_cell)
    return jnp.where(marked, MAXD - 1, values).astype(jnp.int32)


def block_levels(rng, extent, cuts, least, high):
    gain, own = 1.0, jax.random.fold_in(rng, 6)
    for dim, blocks in cuts:
        heights = jnp.exp(jax.random.uniform(jax.random.fold_in(own, dim), (blocks,), jnp.float32, least / len(cuts), high / len(cuts)))
        gain = gain * jnp.repeat(heights, extent[dim] // blocks).reshape([-1 if axis == dim else 1 for axis in range(len(extent))])
    return gain


def gaussian(stream_key, dims, deviation, most, shards=(), kind=jnp.bfloat16):
    loudness = block_levels(stream_key, dims, shards, -0.22, 0.18) if shards else 1.0
    array = jax.random.normal(stream_key, dims, jnp.float32) * deviation * loudness
    return jnp.minimum(jnp.maximum(array, -most), most).astype(kind)


def setup_inputs(seed: int = 0, part: int = 0) -> dict:
    splits = jax.random.split(jax.random.key(seed), 12)
    own_keys = jax.random.split(jax.random.fold_in(splits[11], part), 12)
    left_feat = gaussian(own_keys[0], (IMGS, ROWS, WIDTH, FEAT), 1.0, 6.0, ((2, 16),))
    right_feat = gaussian(own_keys[1], (IMGS, ROWS, WIDTH, FEAT), 1.0, 6.0, ((2, 16),))
    bounds = draw_bounds(jax.random.fold_in(jax.random.fold_in(splits[11], part), 71), part)
    disparity = draw_disparity(jax.random.fold_in(jax.random.fold_in(splits[11], part), 71), part)
    hidden_fine = jnp.clip(jax.random.uniform(own_keys[4], (IMGS, ROWS, WIDTH, HID), jnp.float32, -1.0, 1.0) * block_levels(own_keys[4], (IMGS, ROWS, WIDTH, HID), ((2, 16),), -0.4, 0.0), -1.0, 1.0).astype(jnp.bfloat16)
    hidden_coarse = jnp.clip(jax.random.uniform(own_keys[5], (IMGS, ROWS // 8, WIDTH // 8, HID), jnp.float32, -1.0, 1.0) * block_levels(own_keys[5], (IMGS, ROWS // 8, WIDTH // 8, HID), ((2, 16),), -0.4, 0.0), -1.0, 1.0).astype(jnp.bfloat16)
    motion_weight = gaussian(splits[6], (CORR_CH, HID), CORR_CH ** -0.5, 1.0)
    fine_gates = gaussian(splits[7], (9, 3 * HID, 2 * HID), (9 * 3 * HID) ** -0.5, 0.109375)
    fine_candidate = gaussian(splits[8], (9, 3 * HID, HID), (9 * 3 * HID) ** -0.5, 0.109375)
    coarse_gates = gaussian(splits[9], (9, 2 * HID, 2 * HID), (9 * 2 * HID) ** -0.5, 0.125)
    coarse_candidate = gaussian(splits[10], (9, 2 * HID, HID), (9 * 2 * HID) ** -0.5, 0.125)
    return {"left_feat": left_feat, "right_feat": right_feat, "bounds": bounds, "disparity": disparity, "hidden_fine": hidden_fine, "hidden_coarse": hidden_coarse, "motion_weight": motion_weight, "fine_gates": fine_gates, "fine_candidate": fine_candidate, "coarse_gates": coarse_gates, "coarse_candidate": coarse_candidate}


def convolve(padded, weight):
    images, rows_pad, cols_pad, channels = padded.shape
    rows_out = rows_pad - 2
    cols_out = cols_pad - 2
    summed = jnp.zeros((images * rows_out * cols_out, weight.shape[2]), jnp.float32)
    for row_off in range(3):
        for col_off in range(3):
            window = padded[:, row_off:row_off + rows_out, col_off:col_off + cols_out, :].reshape(-1, channels)
            summed = summed + jnp.dot(window, weight[3 * row_off + col_off], preferred_element_type=jnp.float32)
    return summed.reshape(images, rows_out, cols_out, weight.shape[2])


def pad_rows(field):
    return jnp.pad(field, ((0, 0), (1, 1), (0, 0), (0, 0)))


def wrap_cols(field):
    return jnp.concatenate([field[:, :, -1:], field, field[:, :, :1]], axis=2)


def gru_full(state, extra, gates_weight, cand_weight):
    hidden_width = state.shape[-1]
    gru_input = jnp.concatenate([state, extra], -1)
    gates = jax.nn.sigmoid(convolve(pad_rows(wrap_cols(gru_input)), gates_weight))
    update_gate = gates[..., :hidden_width]
    reset_state = (gates[..., hidden_width:] * state.astype(jnp.float32)).astype(jnp.bfloat16)
    cand_input = jnp.concatenate([reset_state, extra], -1)
    candidate = jnp.tanh(convolve(pad_rows(wrap_cols(cand_input)), cand_weight))
    updated = (1.0 - update_gate) * state.astype(jnp.float32) + update_gate * candidate
    return updated.astype(jnp.bfloat16)


def pyramid_lookup(cost, disparity):
    features = []
    volume = cost
    for octave in range(LEVELS):
        if octave > 0:
            volume = 0.5 * (volume[..., 0::2] + volume[..., 1::2])
        entries = volume.shape[-1]
        center = disparity // (2 ** octave)
        position = center[..., None] + jnp.arange(2 * RADIUS + 1, dtype=jnp.int32) - RADIUS
        inside = (position >= 0) & (position < entries)
        picked = jnp.take_along_axis(volume, jnp.clip(position, 0, entries - 1).astype(jnp.int32), axis=-1)
        features.append(jnp.where(inside, picked, 0.0))
    return jnp.concatenate(features, -1)


def reference(left_feat, right_feat, bounds, disparity, hidden_fine, hidden_coarse, motion_weight, fine_gates, fine_candidate, coarse_gates, coarse_candidate):
    images, rows_all, cols_all, channels = left_feat.shape
    hidden_width = hidden_fine.shape[-1]
    left_wide = left_feat.astype(jnp.float32)
    right_wide = right_feat.astype(jnp.float32)

    def one_disparity(shift_by):
        return jnp.sum(left_wide * jnp.roll(right_wide, shift_by, axis=2), axis=-1)

    cost = lax.map(one_disparity, jnp.arange(MAXD, dtype=jnp.int32))
    cost = jnp.moveaxis(cost, 0, -1) * (channels ** -0.5)
    valid = jnp.arange(MAXD, dtype=jnp.int32)[None, None, None, :] < bounds[:, None, None, None]
    cost = jnp.where(valid, cost, 0.0)
    lookup = pyramid_lookup(cost, disparity).astype(jnp.bfloat16)
    motion = jax.nn.relu(jnp.dot(lookup.reshape(-1, lookup.shape[-1]), motion_weight, preferred_element_type=jnp.float32))
    motion = motion.astype(jnp.bfloat16).reshape(images, rows_all, cols_all, hidden_width)
    pooled = hidden_fine.astype(jnp.float32).reshape(images, rows_all // 8, 8, cols_all // 8, 8, hidden_width)
    pooled = jnp.mean(pooled, axis=(2, 4)).astype(jnp.bfloat16)
    coarse_new = gru_full(hidden_coarse, pooled, coarse_gates, coarse_candidate)
    upsampled = jnp.repeat(jnp.repeat(coarse_new, 8, axis=1), 8, axis=2)
    fine_new = gru_full(hidden_fine, jnp.concatenate([motion, upsampled], -1), fine_gates, fine_candidate)
    return (fine_new, coarse_new)
```

```python
import functools

import jax
import jax.numpy as jnp
import numpy as np
from jax import lax
from jax.experimental import pallas as pl
from jax.experimental.pallas import tpu as pltpu
from jax.sharding import PartitionSpec as P

LEVELS = 4
RADIUS = 4
MAXD = 64
CHUNKS = 2
EDGE = (-2, 15, -1, 16, 0, 17, 0, 0)


def permute(value, target, take=lambda j: True):
    count = lax.axis_size("cols")
    pairs = [(j, target(j) % count) for j in range(count) if take(j)]
    return lax.ppermute(value, "cols", pairs)


def near(value):
    return pltpu.with_memory_space_constraint(value, pltpu.VMEM)


def dot(a, b):
    return jnp.dot(a, b, preferred_element_type=jnp.float32)


def onehot(shape, column):
    r = lax.broadcasted_iota(jnp.int32, shape, 0)
    c = lax.broadcasted_iota(jnp.int32, shape, 1)
    return jnp.where(column(r, c), 1.0, 0.0).astype(jnp.bfloat16)


def call(kernel, name, outs, scratch, args, limit=8, smem=0, **kw):
    vmem = pl.BlockSpec(memory_space=pltpu.VMEM)
    return pl.pallas_call(
        kernel,
        out_shape=tuple(pltpu.VMEM(shape, dtype) for shape, dtype in outs),
        in_specs=[pl.BlockSpec(memory_space=pltpu.SMEM)] * smem + [vmem] * (len(args) - smem),
        out_specs=(vmem,) * len(outs),
        scratch_shapes=scratch,
        compiler_params=pltpu.CompilerParams(vmem_limit_bytes=limit << 20),
        name=name,
        **kw,
    )(*args[:smem], *(near(a) for a in args[smem:]))


def pack_kernel(left, right, state, coarse, disp, to_next, to_prev, far, flat, pooled):
    images, rows, cols, channels = left.shape
    hid = state.shape[-1]
    many = images * rows
    wide = 16 * cols

    def end(q):
        return q + jnp.where(q >= 2, cols - 4, 0)

    ends = onehot((64, wide), lambda r, c: c == (r & 15) * cols + end(r >> 4))
    per_cell = onehot((8, wide), lambda r, c: (r == (c // (8 * cols)) * (cols // 8) + (c % cols) // 8))
    for b in range(many // 16):
        i, r0 = divmod(16 * b, rows)
        here = pl.ds(16 * b, 16)

        def put(ref, slot, value):
            ref[pl.ds(many * slot + 16 * b, 16), :] = value.astype(jnp.bfloat16)

        e = dot(ends, left[i, r0: r0 + 16].reshape(wide, channels))
        put(to_prev, 0, e[:16])
        put(to_prev, 1, e[16:32])
        put(to_next, 0, e[32:48])
        put(to_next, 1, e[48:])
        e = dot(ends, right[i, r0: r0 + 16].reshape(wide, channels))
        put(to_prev, 2, e[:16])
        put(to_prev, 3, e[16:32])
        put(far, 0, e[48:])
        fine = state[i, r0: r0 + 16].reshape(wide, hid)
        e = dot(ends, fine)
        put(to_prev, 4, jnp.concatenate([e[:16], e[16:32]], axis=1))
        put(to_next, 2, jnp.concatenate([e[32:48], e[48:]], axis=1))
        cells = 2 * (cols // 8)
        pooled[pl.ds(cells * b, cells), :] = (dot(per_cell, fine) * (1.0 / 64))[:cells]
    both = jnp.concatenate([coarse[...], pooled[...].astype(jnp.bfloat16)], axis=1)
    flat[...] = both
    to_next[pl.ds(3 * many, flat.shape[0]), :] = both
    to_prev[pl.ds(5 * many, flat.shape[0]), :] = both
    pick = onehot((16, cols), lambda r, c: (c == end(r)) & (r < 4))
    d = lax.dot_general(pick, disp[...].astype(jnp.float32).astype(jnp.bfloat16), (((1,), (1,)), ((), ())),
                        preferred_element_type=jnp.float32)
    d = jnp.concatenate([d, jnp.zeros((16, channels - many), jnp.float32)], axis=1).astype(jnp.bfloat16)
    to_next[pl.ds(3 * many + flat.shape[0], 16), :] = d
    to_prev[pl.ds(5 * many + flat.shape[0], 16), :] = d


def edge_kernel(prev, foll, far, to_next, to_prev, state, disp, left_edge, right_edge, disp24, hid_edge, hid3, wide):
    images, rows, cols, hid = state.shape
    many = images * rows
    channels = prev.shape[1]
    last = prev.shape[0] - 16
    spread8 = onehot((128, 96), lambda r, c: c == (r & 7) * 16 + (r >> 3))
    spread16 = onehot((256, 48), lambda r, c: c == jnp.where((r & 15) == 15, 2, jnp.where((r & 15) < 2, r & 15, 9)) * 16 + (r >> 4))

    own = disp[...].astype(jnp.float32).astype(jnp.bfloat16)
    d24 = dot(own, onehot((cols, cols + 8), lambda r, c: (r == c) | ((c == cols + 1) & (r == cols - 1))
                          | ((c == cols + 4) & (r == 0))))
    for ref, first, slots in ((prev, last, ((2, 0), (3, 2))), (foll, foll.shape[0] - 16, ((0, 3), (1, 5)))):
        rows16 = ref[pl.ds(first, 16), :many]
        place = onehot((16, cols + 8), lambda r, c: ((r == slots[0][0]) & (c == cols + slots[0][1]))
                       | ((r == slots[1][0]) & (c == cols + slots[1][1])))
        d24 += lax.dot_general(rows16, place, (((0,), (0,)), ((), ())), preferred_element_type=jnp.float32)
    d24 = d24.astype(jnp.bfloat16)
    slots = cols + 8
    repeat = onehot((16 * slots, 16), lambda r, c: c == r // slots)
    match = lax.broadcasted_iota(jnp.int32, (16 * slots, slots), 0) % slots \
        == lax.broadcasted_iota(jnp.int32, (16 * slots, slots), 1)
    ones = jnp.ones((slots, 128), jnp.bfloat16)

    for i in range(images):
        for line in (0, rows + 1):
            hid3[i, line] = jnp.zeros((cols, 3 * hid), jnp.bfloat16)
            hid_edge[i, pl.ds(8 * line, 8), :] = jnp.zeros((8, hid), jnp.float32)
    for b in range(many // 16):
        i, r0 = divmod(16 * b, rows)

        def get(ref, slot):
            return ref[pl.ds(many * slot + 16 * b, 16), :]

        e = dot(spread8, jnp.concatenate([get(prev, 0), get(to_next, 1), get(prev, 1), get(foll, 0), get(to_prev, 0),
                                          get(foll, 1)], axis=0))
        left_edge[i, r0: r0 + 16] = e.reshape(16, 8, channels).astype(jnp.bfloat16)
        e = dot(spread16, jnp.concatenate([get(foll, 2), get(foll, 3), get(far, 0)], axis=0))
        right_edge[i, r0: r0 + 16] = e.reshape(16, 16, channels).astype(jnp.bfloat16)
        hp, hn, on, op = get(prev, 2), get(foll, 4), get(to_next, 2), get(to_prev, 4)
        e = dot(spread8, jnp.concatenate([hp[:, :hid], on[:, hid:], hp[:, hid:], hn[:, :hid], op[:, :hid], hn[:, hid:]],
                                         axis=0))
        hid_edge[i, pl.ds(8 + 8 * r0, 128), :] = e
        for k in range(16):
            wide[pl.ds(32 * k + 8, cols), :] = state[i, r0 + k].astype(jnp.float32)
        wide[pl.ds(7, 16, stride=32), :] = hp[:, hid:].astype(jnp.float32)
        wide[pl.ds(8 + cols, 16, stride=32), :] = hn[:, :hid].astype(jnp.float32)
        for k in range(16):
            hid3[i, 1 + r0 + k] = jnp.concatenate(
                [wide[pl.ds(32 * k + 7 + t, cols), :].astype(jnp.bfloat16) for t in range(3)], axis=1)
        spread = jnp.where(match, dot(repeat, d24[16 * b: 16 * b + 16]), 0.0).astype(jnp.bfloat16)
        disp24[i, r0: r0 + 16] = dot(spread, ones).astype(jnp.int32).reshape(16, slots, 128)


def coarse_kernel(behind2, prev, flat, foll, ahead2, gates, cand, fine_gates, fine_cand, new, up_z, up_r, up_q, up_edge,
                  columns, shifted, scratch):
    count = flat.shape[0]
    cells = count // 2
    hid = new.shape[1]
    images = up_edge.shape[0]
    tall = cells // images

    def moved(value, by):
        row = lax.broadcasted_iota(jnp.int32, value.shape, 0) % tall
        if by > 0:
            return jnp.where(row == 0, 0.0, pltpu.roll(value, 1, 0))
        return jnp.where(row == tall - 1, 0.0, pltpu.roll(value, value.shape[0] - 1, 0))

    many3, many5 = prev.shape[0] - 16 - count, foll.shape[0] - 16 - count
    sources = (behind2[...], prev[pl.ds(many3, count), :], flat[...], foll[pl.ds(many5, count), :], ahead2[...])
    for n, source in enumerate(sources):
        for half in range(2):
            columns[half, pl.ds(count * n, count), :] = source[:, half * hid:(half + 1) * hid].astype(jnp.float32)
    state = []
    for n in range(8):
        parts = [columns[half, pl.ds(count * ((n + 1) // 2) + (n + 1) % 2, cells, stride=2), :] for half in range(2)]
        state.append(parts[0])
        both = jnp.concatenate(parts, axis=1)
        for a in range(3):
            value = both if a == 1 else moved(both, 1 - a)
            shifted[a, pl.ds(cells * n, cells), :] = value.astype(jnp.bfloat16)
    acc = jnp.zeros((6 * cells, 2 * hid), jnp.float32)
    for a in range(3):
        for b in range(3):
            acc += dot(shifted[a, pl.ds(cells * b, 6 * cells), :], gates[3 * a + b])
    zr = jax.nn.sigmoid(acc)
    reset = zr[:, hid:] * jnp.concatenate(state[1:7], axis=0)
    reset = reset.astype(jnp.bfloat16).astype(jnp.float32)
    acc = jnp.zeros((4 * cells, hid), jnp.float32)
    for a in range(3):
        value = (reset if a == 1 else moved(reset, 1 - a)).astype(jnp.bfloat16)
        for b in range(3):
            lhs = jnp.concatenate([value[cells * b: cells * (b + 4)],
                                   shifted[a, pl.ds(cells * (b + 1), 4 * cells), hid:]], axis=1)
            acc += dot(lhs, cand[3 * a + b])
    q = jnp.tanh(acc)
    z = zr[cells: 5 * cells, :hid]
    fresh = (1.0 - z) * jnp.concatenate(state[2:6], axis=0) + z * q
    rounded = fresh.astype(jnp.bfloat16)
    for n in range(2):
        scratch[pl.ds(n, cells, stride=2), :] = fresh[cells * (n + 1): cells * (n + 2)]
    new[...] = scratch[...].astype(jnp.bfloat16)

    sums = []
    for b in range(3):
        p = []
        for a in range(3):
            w = jnp.concatenate([fine_gates[3 * a + b, 2 * hid:, :], fine_cand[3 * a + b, 2 * hid:, :]], axis=1)
            p.append(dot(rounded, w))
        low = p[0] + p[1]
        sums.append((moved(p[0], 1) + p[1] + p[2], low + p[2], low + moved(p[2], -1)))

    def at(kind, js):
        return sum(sums[b][kind][cells * (js[b] + 1): cells * (js[b] + 2)] for b in range(3))

    for kind in range(3):
        inner = {0: (-1, 0, 0), 7: (0, 0, 1), 8: (0, 1, 1), 15: (1, 1, 2)}
        flat0, flat1 = at(kind, (0, 0, 0)), at(kind, (1, 1, 1))
        for x in range(16):
            value = at(kind, inner[x]) if x in inner else (flat0 if x < 8 else flat1)
            for part, ref in enumerate((up_z, up_r, up_q)):
                ref[pl.ds(kind * 16 + x, cells, stride=48), :] = value[:, part * hid:(part + 1) * hid]
        for side, js in enumerate(((-1, -1, 0), (1, 2, 2))):
            value = at(kind, js)[:, hid: 2 * hid]
            for i in range(images):
                for u in ((0,), range(1, 7), (7,))[kind]:
                    up_edge[i, pl.ds(side * 8 * tall + u, tall, stride=8), :] = value[tall * i: tall * (i + 1)]


def corr_kernel(sc, left, left_edge, right, right_edge, b4, b2, d2, d0, d4, disp, distance, start, table,
                mot3, mot_edge, wide):
    rows = right.shape[0]
    group = 8
    even = sc[1] == 1
    known = (distance[...] >= 0) & (distance[...] < sc[0])
    scale = jnp.where(known, jnp.float32(left.shape[-1] ** -0.5), 0.0)
    lane = lax.broadcasted_iota(jnp.int32, (24, 128), 1)
    keep = (jnp.where(lane < 72, ~7, ~3), jnp.where(lane < 18, ~1, ~0))
    last_lane = lax.broadcasted_iota(jnp.int32, (8, 128), 1) == 127

    def body(g, carry):
        scores, places = [], ([], [])
        for k in range(group):
            h = g * group + k
            b1 = jnp.where(even, d2[h], d0[h])
            b3 = jnp.where(even, d4[h], d2[h])
            window = jnp.concatenate([b4[h], b3, b2[h], b1, right[h], right_edge[h]], axis=0)
            pixels = jnp.concatenate([left[h], left_edge[h]], axis=0)
            s = lax.dot_general(pixels, window, (((1,), (1,)), ((), ())), preferred_element_type=jnp.float32)
            s = jnp.concatenate([s, jnp.zeros((s.shape[0], 128 - s.shape[1]), jnp.float32)], axis=1)
            ends = jnp.where(last_lane, pltpu.roll(s[16:], 32, 1), s[16:])
            scores.append(s[:16] * scale[:16])
            scores.append(ends * scale[16:])
            d = disp[h]
            for n in range(2):
                places[n].append((start[n] - (d & keep[n])) & 127)
        c = jnp.concatenate(scores, axis=0)
        found = [jnp.take_along_axis(c, jnp.concatenate(p, axis=0), axis=1, mode="promise_in_bounds") for p in places]
        motion = jnp.maximum(dot(jnp.concatenate(found, axis=1).astype(jnp.bfloat16), table[...]), 0.0)
        for k in range(group):
            h = g * group + k
            m = motion[24 * k: 24 * k + 24]
            wide[pl.ds(32 * k + 8, 16), :] = m[:16]
            mot_edge[h] = m[16:]
            wide[pl.ds(32 * k + 7, 1), :] = m[18:19]
            wide[pl.ds(32 * k + 24, 1), :] = m[19:20]
        for k in range(group):
            h = g * group + k
            mot3[h] = jnp.concatenate(
                [wide[pl.ds(32 * k + 7 + b, 16), :].astype(jnp.bfloat16) for b in range(3)], axis=1)
        return carry

    lax.fori_loop(0, rows // group, body, 0)


def motion_chunk(i, k, sc, left, left_edge, right, right_edge, b4, b2, d2, d0, d4, disp, distance, start, table):
    rows = b4.shape[0]
    hid = table.shape[1]

    def kernel(sc, left, left_edge, right, right_edge, b4, b2, d2, d0, d4, disp, *rest):
        here = pl.ds(k * rows, rows)
        corr_kernel(sc, left.at[i, here], left_edge.at[i, here], right.at[i, here], right_edge.at[i, here],
                    b4, b2, d2, d0.at[here], d4, disp.at[i, here], *rest)

    return call(kernel, "motion", [((rows, 16, 3 * hid), jnp.bfloat16), ((rows, 8, hid), jnp.float32)],
                [pltpu.VMEM((8 * 32, hid), jnp.float32)],
                (sc, left, left_edge, right, right_edge, b4, b2, d2, d0, d4, disp, distance, start, table), smem=1)


def gru_kernel(count, hid3, state, hid_edge, *refs):
    mots, edges = refs[:count], refs[count:2 * count]
    (up_z, up_r, up_q, up_edge, gates, cand, out, mot, mot_edge, z_keep, wide, res3) = refs[2 * count:]
    rows = state.shape[0]
    hid = state.shape[-1]
    each = rows // count
    zero = jnp.zeros((1, 16, 3 * hid), jnp.bfloat16)
    mot[0:1] = zero
    mot[rows + 1: rows + 2] = zero
    res3[0:1] = zero
    res3[rows + 1: rows + 2] = zero
    mot_edge[0:8] = jnp.zeros((8, hid), jnp.float32)
    mot_edge[8 * (rows + 1): 8 * (rows + 2)] = jnp.zeros((8, hid), jnp.float32)
    for k in range(count):
        mot[1 + each * k: 1 + each * (k + 1)] = mots[k][...]
        mot_edge[8 + 8 * each * k: 8 + 8 * each * (k + 1)] = edges[k][...].reshape(8 * each, hid)
    block = 16

    acc = up_edge[...]
    for a in range(3):
        for b in range(3):
            pieces = [
                jnp.concatenate([src[pl.ds(8 * a + 2 * b + side, rows, stride=8), :] for side in range(2)], axis=0)
                for src in (hid_edge, mot_edge)]
            acc += dot(jnp.concatenate(pieces, axis=1).astype(jnp.bfloat16),
                       gates[3 * a + b, 0: 2 * hid, hid: 2 * hid])
    centre = jnp.concatenate([hid_edge[pl.ds(8 + 2 + side, rows, stride=8), :] for side in range(2)], axis=0)
    reset = jax.nn.sigmoid(acc) * centre
    wide[pl.ds(7, rows, stride=32), :] = reset[:rows]
    wide[pl.ds(24, rows, stride=32), :] = reset[rows:]

    def taps(first, weights, source, r0, start):
        acc = start
        for a in range(3):
            one = source[pl.ds(r0 + a, block)].reshape(block * 16, 3 * hid)
            two = mot[pl.ds(r0 + a, block)].reshape(block * 16, 3 * hid)
            for b in range(3):
                lhs = jnp.concatenate([one[:, b * hid:(b + 1) * hid], two[:, b * hid:(b + 1) * hid]], axis=1)
                acc += dot(lhs, weights[3 * a + b, 0: 2 * hid, :])
        return acc

    def upsampled(g, *refs):
        parts = []
        for cell in range(block // 8):
            kinds = [jnp.concatenate([ref[g * (block // 8) + cell, kind] for ref in refs], axis=1) for kind in range(3)]
            parts += [kinds[0]] + [kinds[1]] * 6 + [kinds[2]]
        return jnp.concatenate(parts, axis=0)

    def gate_body(g, carry):
        r0 = g * block
        acc = taps(0, gates, hid3, r0, upsampled(g, up_z, up_r))
        both = jax.nn.sigmoid(acc)
        h = state[pl.ds(r0, block)].reshape(block * 16, hid).astype(jnp.float32)
        z_keep[pl.ds(r0 * 16, block * 16), :] = both[:, :hid]
        reset = both[:, hid:] * h
        for k in range(block):
            wide[pl.ds(pl.multiple_of((r0 + k) * 32, 32) + 8, 16), :] = reset[16 * k: 16 * k + 16]
        for k in range(block):
            res3[r0 + k + 1] = jnp.concatenate(
                [wide[pl.ds(pl.multiple_of((r0 + k) * 32, 32) + 7 + b, 16), :].astype(jnp.bfloat16)
                 for b in range(3)], axis=1)
        return carry

    lax.fori_loop(0, rows // block, gate_body, 0)

    def cand_body(g, carry):
        r0 = g * block
        q = jnp.tanh(taps(0, cand, res3, r0, upsampled(g, up_q)))
        h = state[pl.ds(r0, block)].reshape(block * 16, hid).astype(jnp.float32)
        z = z_keep[pl.ds(r0 * 16, block * 16), :]
        new = (1.0 - z) * h + z * q
        out[pl.ds(r0, block)] = new.astype(jnp.bfloat16).reshape(block, 16, hid)
        return carry

    lax.fori_loop(0, rows // block, cand_body, 0)


def fine_gru(i, before, hid3, state, hid_edge, mots, edges, ups, up_edge, gates, cand):
    images, rows, cols, hid = state.shape
    count = len(mots)
    vmem = pl.BlockSpec(memory_space=pltpu.VMEM)
    tall = rows // 8

    def kernel(hid3, state, hid_edge, *refs):
        refs = list(refs)
        if before is not None:
            refs = refs[1:]
        for n in range(3):
            refs[2 * count + n] = refs[2 * count + n].at[pl.ds(tall * i, tall)]
        refs[2 * count + 3] = refs[2 * count + 3].at[i]
        gru_kernel(count, hid3.at[i], state.at[i], hid_edge.at[i], *refs)

    args = [hid3, state, hid_edge]
    rest = [*mots, *edges, *(u.reshape(-1, 3, 16, hid) for u in ups), up_edge, gates, cand]
    first = [] if before is None else [before]
    return pl.pallas_call(
        kernel,
        grid=(1,),
        out_shape=jax.ShapeDtypeStruct(state.shape, jnp.bfloat16),
        in_specs=[vmem] * 3 + [pl.BlockSpec(memory_space=pl.ANY)] * len(first) + [vmem] * len(rest),
        out_specs=pl.BlockSpec((None, rows, cols, hid), lambda _: (i, 0, 0, 0)),
        input_output_aliases={3: 0} if first else {},
        compiler_params=pltpu.CompilerParams(vmem_limit_bytes=16 << 20),
        scratch_shapes=[pltpu.VMEM((rows + 2, 16, 3 * hid), jnp.bfloat16),
                        pltpu.VMEM((8 * (rows + 2), hid), jnp.float32),
                        pltpu.VMEM((rows * 16, hid), jnp.float32),
                        pltpu.VMEM((rows * 32, hid), jnp.float32),
                        pltpu.VMEM((rows + 2, 16, 3 * hid), jnp.bfloat16)],
        name="fine_gru",
    )(*(near(v) for v in args), *first, *(near(v) for v in rest))


def lookup_places():
    level = np.full((2, 128), -1)
    offset = np.zeros((2, 128), np.int64)
    for group, first, k in ((0, 0, 3), (0, 72, 2), (1, 0, 1), (1, 18, 0)):
        count = (2 * RADIUS + 1) << k
        level[group, first: first + count] = k
        offset[group, first: first + count] = ((RADIUS + 1) << k) - 1 - np.arange(count)
    tap = np.where(level >= 0, (offset >> np.maximum(level, 0)) + RADIUS, 0)
    return level, offset, tap


def lookup_table(motion_weight):
    level, _, tap = (v.reshape(-1) for v in lookup_places())
    rows = np.maximum(level, 0) * (2 * RADIUS + 1) + tap
    pick = np.zeros((level.size, motion_weight.shape[0]), np.float32)
    pick[np.arange(level.size), rows] = np.where(level >= 0, 0.5 ** np.maximum(level, 0), 0.0)
    return dot(jnp.asarray(pick.astype(jnp.bfloat16)), motion_weight).astype(jnp.bfloat16)


def local(left_feat, right_feat, bounds, disparity, hidden_fine, hidden_coarse, motion_weight,
          fine_gates, fine_candidate, coarse_gates, coarse_candidate):
    images, rows, cols, channels = left_feat.shape
    hid = hidden_fine.shape[-1]
    even = 1 - lax.rem(lax.axis_index("cols"), 2)
    many = images * rows
    each = rows // CHUNKS
    keys = [(i, k) for i in range(images) for k in range(CHUNKS)]
    bf16, f32 = jnp.bfloat16, jnp.float32

    b4, b2, d2, d4 = {}, {}, {}, {}
    for i, k in keys:
        b4[i, k] = permute(right_feat[i, k * each:(k + 1) * each], lambda j: j + 4)
    d0 = [permute(right_feat[i], lambda j: j + 1, lambda j: j % 2 == 0) for i in range(images)]
    straight = [permute(right_feat[i], lambda j: j + 2, lambda j: j % 4 < 2) for i in range(images)]

    disp = disparity.reshape(many, cols)
    cells = hidden_coarse.shape[1] * hidden_coarse.shape[2] * images
    to_next, to_prev, to_far, flat = call(
        pack_kernel, "pack",
        [((3 * many + cells + 16, channels), bf16), ((5 * many + cells + 16, channels), bf16), ((many, channels), bf16),
         ((cells, channels), bf16)],
        [pltpu.VMEM((cells, hid), f32)],
        (left_feat, right_feat, hidden_fine, hidden_coarse.reshape(-1, hid), disp))
    prev = permute(to_next, lambda j: j + 1)
    foll = permute(to_prev, lambda j: j - 1)
    far = permute(to_far, lambda j: j + 5)
    behind2 = permute(flat, lambda j: j + 2)
    ahead2 = permute(flat, lambda j: j - 2)

    for i, k in keys:
        relayed = permute(b4[i, k], lambda j: j - 2, lambda j: j % 4 >= 2)
        b2[i, k] = straight[i][k * each:(k + 1) * each] + relayed
        d4[i, k] = permute(b4[i, k], lambda j: j - 1, lambda j: j % 2 == 1)
        d2[i, k] = permute(b2[i, k], lambda j: j ^ 1)

    left_edge, right_edge, disp24, hid_edge, hid3 = call(
        edge_kernel, "edges",
        [((images, rows, 8, channels), bf16), ((images, rows, 16, channels), bf16), ((images, rows, 24, 128), jnp.int32),
         ((images, 8 * (rows + 2), hid), f32), ((images, rows + 2, cols, 3 * hid), bf16)],
        [pltpu.VMEM((16 * 32, hid), f32)],
        (prev, foll, far, to_next, to_prev, hidden_fine, disp))
    new, *ups, up_edge = call(
        coarse_kernel, "coarse",
        [((cells, hid), bf16)] + [((cells // 2 * 48, hid), f32)] * 3 + [((images, 2 * rows, hid), f32)],
        [pltpu.VMEM((2, 5 * cells, hid), f32), pltpu.VMEM((3, 4 * cells, 2 * hid), bf16), pltpu.VMEM((cells, hid), f32)],
        (behind2, prev, flat, foll, ahead2, coarse_gates, coarse_candidate, fine_gates, fine_candidate))
    coarse_new = new.reshape(hidden_coarse.shape)

    where_x = np.array(list(range(cols)) + list(EDGE), np.int32)[:, None]
    lane = np.arange(128, dtype=np.int32)[None]
    column_of = np.where(lane == 127, -65, np.where(lane < 82, lane - 64, 1000))
    distance = where_x - column_of
    distance = jnp.asarray(np.where((distance >= 0) & (distance < MAXD), distance, -1).astype(np.int32))
    _, offset, _ = lookup_places()
    start = jnp.asarray((where_x + 64 - offset[:, None, :]).astype(np.int32))
    table = lookup_table(motion_weight)

    fine = None
    for i in range(images):
        sc = jnp.stack([bounds[i], even]).astype(jnp.int32)
        done = [motion_chunk(i, k, sc, left_feat, left_edge, right_feat, right_edge, b4[i, k], b2[i, k], d2[i, k], d0[i],
                             d4[i, k], disp24, distance, start, table) for k in range(CHUNKS)]
        fine = fine_gru(i, fine, hid3, hidden_fine, hid_edge, [m for m, _ in done], [e for _, e in done],
                        ups, up_edge, fine_gates, fine_candidate)
    return (fine, coarse_new)


def solution(mesh):
    return jax.shard_map(
        local,
        mesh=mesh,
        in_specs=(
            P("groups", None, "cols", None),
            P("groups", None, "cols", None),
            P("groups"),
            P("groups", None, "cols"),
            P("groups", None, "cols", None),
            P("groups", None, "cols", None),
            P(),
            P(),
            P(),
            P(),
            P(),
        ),
        out_specs=(P("groups", None, "cols", None), P("groups", None, "cols", None)),
        check_vma=False,
    )
```

```python
import functools

import jax
import jax.numpy as jnp
import numpy as np
from jax import lax
from jax.experimental import pallas as pl
from jax.experimental.pallas import tpu as pltpu
from jax.sharding import PartitionSpec as P

LEVELS = 4
RADIUS = 4
MAXD = 64
CHUNKS = 2
EDGE = (-2, 15, -1, 16, 0, 17, 0, 0)


def permute(value, target, take=lambda j: True):
    count = lax.axis_size("cols")
    pairs = [(j, target(j) % count) for j in range(count) if take(j)]
    return lax.ppermute(value, "cols", pairs)


def near(value):
    return pltpu.with_memory_space_constraint(value, pltpu.VMEM)


def dot(a, b):
    return jnp.dot(a, b, preferred_element_type=jnp.float32)


def onehot(shape, column):
    r = lax.broadcasted_iota(jnp.int32, shape, 0)
    c = lax.broadcasted_iota(jnp.int32, shape, 1)
    return jnp.where(column(r, c), 1.0, 0.0).astype(jnp.bfloat16)


def cost(us):
    return pl.CostEstimate(flops=0, bytes_accessed=int(us * 3.5e6), transcendentals=0)


def call(kernel, name, outs, scratch, args, us, limit=8, smem=0, **kw):
    vmem = pl.BlockSpec(memory_space=pltpu.VMEM)
    return pl.pallas_call(
        kernel,
        out_shape=tuple(pltpu.VMEM(shape, dtype) for shape, dtype in outs),
        in_specs=[pl.BlockSpec(memory_space=pltpu.SMEM)] * smem + [vmem] * (len(args) - smem),
        out_specs=(vmem,) * len(outs),
        scratch_shapes=scratch,
        compiler_params=pltpu.CompilerParams(vmem_limit_bytes=limit << 20),
        name=name,
        cost_estimate=cost(us),
        **kw,
    )(*args[:smem], *(near(a) for a in args[smem:]))


def pack_kernel(count, left, *refs):
    rights = refs[:count]
    state, coarse, disp, to_next, to_prev, far, flat, pooled = refs[count:]
    images, rows, cols, channels = left.shape
    hid = state.shape[-1]
    many = images * rows
    wide = 16 * cols
    each = many // count

    def end(q):
        return q + jnp.where(q >= 2, cols - 4, 0)

    ends = onehot((64, wide), lambda r, c: c == (r & 15) * cols + end(r >> 4))
    per_cell = onehot((8, wide), lambda r, c: (r == (c // (8 * cols)) * (cols // 8) + (c % cols) // 8))
    for b in range(many // 16):
        i, r0 = divmod(16 * b, rows)
        here = pl.ds(16 * b, 16)

        def put(ref, slot, value):
            ref[pl.ds(many * slot + 16 * b, 16), :] = value.astype(jnp.bfloat16)

        e = dot(ends, left[i, r0: r0 + 16].reshape(wide, channels))
        put(to_prev, 0, e[:16])
        put(to_prev, 1, e[16:32])
        put(to_next, 0, e[32:48])
        put(to_next, 1, e[48:])
        e = dot(ends, rights[16 * b // each][16 * b % each: 16 * b % each + 16].reshape(wide, channels))
        put(to_prev, 2, e[:16])
        put(to_prev, 3, e[16:32])
        put(far, 0, e[48:])
        fine = state[i, r0: r0 + 16].reshape(wide, hid)
        e = dot(ends, fine)
        put(to_prev, 4, jnp.concatenate([e[:16], e[16:32]], axis=1))
        put(to_next, 2, jnp.concatenate([e[32:48], e[48:]], axis=1))
        cells = 2 * (cols // 8)
        pooled[pl.ds(cells * b, cells), :] = (dot(per_cell, fine) * (1.0 / 64))[:cells]
    both = jnp.concatenate([coarse[...], pooled[...].astype(jnp.bfloat16)], axis=1)
    flat[...] = both
    to_next[pl.ds(3 * many, flat.shape[0]), :] = both
    to_prev[pl.ds(5 * many, flat.shape[0]), :] = both
    pick = onehot((16, cols), lambda r, c: (c == end(r)) & (r < 4))
    d = lax.dot_general(pick, disp[...].astype(jnp.float32).astype(jnp.bfloat16), (((1,), (1,)), ((), ())),
                        preferred_element_type=jnp.float32)
    d = jnp.concatenate([d, jnp.zeros((16, channels - many), jnp.float32)], axis=1).astype(jnp.bfloat16)
    to_next[pl.ds(3 * many + flat.shape[0], 16), :] = d
    to_prev[pl.ds(5 * many + flat.shape[0], 16), :] = d


def edge_kernel(bounds, prev, foll, far, to_next, to_prev, state, disp, pick, motion_weight, distance, left_edge, right_edge, disp24, hid_edge,
                hid3, table, scale, wide):
    table[...] = dot(pick[...], motion_weight[...]).astype(jnp.bfloat16)
    images, rows, cols, hid = state.shape
    many = images * rows
    channels = prev.shape[1]
    for i in range(images):
        known = (distance[...] >= 0) & (distance[...] < bounds[i])
        scale[i] = jnp.where(known, jnp.float32(channels ** -0.5), 0.0)
    last = prev.shape[0] - 16
    spread8 = onehot((128, 96), lambda r, c: c == (r & 7) * 16 + (r >> 3))
    spread16 = onehot((256, 48), lambda r, c: c == jnp.where((r & 15) == 15, 2, jnp.where((r & 15) < 2, r & 15, 9)) * 16 + (r >> 4))

    own = disp[...].astype(jnp.float32).astype(jnp.bfloat16)
    d24 = dot(own, onehot((cols, cols + 8), lambda r, c: (r == c) | ((c == cols + 1) & (r == cols - 1))
                          | ((c == cols + 4) & (r == 0))))
    for ref, first, slots in ((prev, last, ((2, 0), (3, 2))), (foll, foll.shape[0] - 16, ((0, 3), (1, 5)))):
        rows16 = ref[pl.ds(first, 16), :many]
        place = onehot((16, cols + 8), lambda r, c: ((r == slots[0][0]) & (c == cols + slots[0][1]))
                       | ((r == slots[1][0]) & (c == cols + slots[1][1])))
        d24 += lax.dot_general(rows16, place, (((0,), (0,)), ((), ())), preferred_element_type=jnp.float32)
    d24 = d24.astype(jnp.bfloat16)
    slots = cols + 8
    repeat = onehot((16 * slots, 16), lambda r, c: c == r // slots)
    match = lax.broadcasted_iota(jnp.int32, (16 * slots, slots), 0) % slots \
        == lax.broadcasted_iota(jnp.int32, (16 * slots, slots), 1)
    ones = jnp.ones((slots, 128), jnp.bfloat16)

    for i in range(images):
        for line in (0, rows + 1):
            hid3[i, line] = jnp.zeros((cols, 3 * hid), jnp.bfloat16)
            hid_edge[i, pl.ds(8 * line, 8), :] = jnp.zeros((8, hid), jnp.float32)
    for b in range(many // 16):
        i, r0 = divmod(16 * b, rows)

        def get(ref, slot):
            return ref[pl.ds(many * slot + 16 * b, 16), :]

        e = dot(spread8, jnp.concatenate([get(prev, 0), get(to_next, 1), get(prev, 1), get(foll, 0), get(to_prev, 0),
                                          get(foll, 1)], axis=0))
        left_edge[i, r0: r0 + 16] = e.reshape(16, 8, channels).astype(jnp.bfloat16)
        e = dot(spread16, jnp.concatenate([get(foll, 2), get(foll, 3), get(far, 0)], axis=0))
        right_edge[i, r0: r0 + 16] = e.reshape(16, 16, channels).astype(jnp.bfloat16)
        hp, hn, on, op = get(prev, 2), get(foll, 4), get(to_next, 2), get(to_prev, 4)
        e = dot(spread8, jnp.concatenate([hp[:, :hid], on[:, hid:], hp[:, hid:], hn[:, :hid], op[:, :hid], hn[:, hid:]],
                                         axis=0))
        hid_edge[i, pl.ds(8 + 8 * r0, 128), :] = e
        for k in range(16):
            wide[pl.ds(32 * k + 8, cols), :] = state[i, r0 + k].astype(jnp.float32)
        wide[pl.ds(7, 16, stride=32), :] = hp[:, hid:].astype(jnp.float32)
        wide[pl.ds(8 + cols, 16, stride=32), :] = hn[:, :hid].astype(jnp.float32)
        for k in range(16):
            hid3[i, 1 + r0 + k] = jnp.concatenate(
                [wide[pl.ds(32 * k + 7 + t, cols), :].astype(jnp.bfloat16) for t in range(3)], axis=1)
        spread = jnp.where(match, dot(repeat, d24[16 * b: 16 * b + 16]), 0.0).astype(jnp.bfloat16)
        disp24[i, r0: r0 + 16] = dot(spread, ones).astype(jnp.int32).reshape(16, slots, 128)


def coarse_kernel(behind2, prev, flat, foll, ahead2, gates, cand, fine_gates, fine_cand, new, up_z, up_r, up_q, up_edge,
                  columns, shifted, scratch):
    count = flat.shape[0]
    cells = count // 2
    hid = new.shape[1]
    images = up_edge.shape[0]
    tall = cells // images

    def moved(value, by):
        row = lax.broadcasted_iota(jnp.int32, value.shape, 0) % tall
        if by > 0:
            return jnp.where(row == 0, 0.0, pltpu.roll(value, 1, 0))
        return jnp.where(row == tall - 1, 0.0, pltpu.roll(value, value.shape[0] - 1, 0))

    many3, many5 = prev.shape[0] - 16 - count, foll.shape[0] - 16 - count
    sources = (behind2[...], prev[pl.ds(many3, count), :], flat[...], foll[pl.ds(many5, count), :], ahead2[...])
    for n, source in enumerate(sources):
        for half in range(2):
            columns[half, pl.ds(count * n, count), :] = source[:, half * hid:(half + 1) * hid].astype(jnp.float32)
    state = []
    for n in range(8):
        parts = [columns[half, pl.ds(count * ((n + 1) // 2) + (n + 1) % 2, cells, stride=2), :] for half in range(2)]
        state.append(parts[0])
        both = jnp.concatenate(parts, axis=1)
        for a in range(3):
            value = both if a == 1 else moved(both, 1 - a)
            shifted[a, pl.ds(cells * n, cells), :] = value.astype(jnp.bfloat16)
    acc = jnp.zeros((6 * cells, 2 * hid), jnp.float32)
    for a in range(3):
        for b in range(3):
            acc += dot(shifted[a, pl.ds(cells * b, 6 * cells), :], gates[3 * a + b])
    zr = jax.nn.sigmoid(acc)
    reset = zr[:, hid:] * jnp.concatenate(state[1:7], axis=0)
    reset = reset.astype(jnp.bfloat16).astype(jnp.float32)
    acc = jnp.zeros((4 * cells, hid), jnp.float32)
    for a in range(3):
        value = (reset if a == 1 else moved(reset, 1 - a)).astype(jnp.bfloat16)
        for b in range(3):
            lhs = jnp.concatenate([value[cells * b: cells * (b + 4)],
                                   shifted[a, pl.ds(cells * (b + 1), 4 * cells), hid:]], axis=1)
            acc += dot(lhs, cand[3 * a + b])
    q = jnp.tanh(acc)
    z = zr[cells: 5 * cells, :hid]
    fresh = (1.0 - z) * jnp.concatenate(state[2:6], axis=0) + z * q
    rounded = fresh.astype(jnp.bfloat16)
    for n in range(2):
        scratch[pl.ds(n, cells, stride=2), :] = fresh[cells * (n + 1): cells * (n + 2)]
    new[...] = scratch[...].astype(jnp.bfloat16)

    sums = []
    for b in range(3):
        p = []
        for a in range(3):
            w = jnp.concatenate([fine_gates[3 * a + b, 2 * hid:, :], fine_cand[3 * a + b, 2 * hid:, :]], axis=1)
            p.append(dot(rounded, w))
        low = p[0] + p[1]
        sums.append((moved(p[0], 1) + p[1] + p[2], low + p[2], low + moved(p[2], -1)))

    def at(kind, js):
        return sum(sums[b][kind][cells * (js[b] + 1): cells * (js[b] + 2)] for b in range(3))

    for kind in range(3):
        inner = {0: (-1, 0, 0), 7: (0, 0, 1), 8: (0, 1, 1), 15: (1, 1, 2)}
        flat0, flat1 = at(kind, (0, 0, 0)), at(kind, (1, 1, 1))
        for x in range(16):
            value = at(kind, inner[x]) if x in inner else (flat0 if x < 8 else flat1)
            for part, ref in enumerate((up_z, up_r, up_q)):
                ref[pl.ds(kind * 16 + x, cells, stride=48), :] = value[:, part * hid:(part + 1) * hid]
        for side, js in enumerate(((-1, -1, 0), (1, 2, 2))):
            value = at(kind, js)[:, hid: 2 * hid]
            for i in range(images):
                for u in ((0,), range(1, 7), (7,))[kind]:
                    up_edge[i, pl.ds(side * 8 * tall + u, tall, stride=8), :] = value[tall * i: tall * (i + 1)]


def copy_either(second_wanted, first, second, out):
    @pl.when(jnp.logical_not(second_wanted))
    def _():
        out[...] = first[...]

    @pl.when(second_wanted)
    def _():
        out[...] = second[...]


def choose_kernel(mine, came, out):
    copy_either(lax.rem(lax.axis_index("cols"), 4) >= 2, mine, came, out)


def choose(mine, came):
    return call(choose_kernel, "choose", [(mine.shape, mine.dtype)], [], (mine, came), 0.2)[0]


def join_kernel(second, mine, came, out):
    out[0] = second[...]
    copy_either(lax.rem(lax.axis_index("cols"), 2) == 1, mine, came, out.at[1])


def join(second, mine, came):
    return call(join_kernel, "join", [((2,) + mine.shape, mine.dtype)], [], (second, mine, came), 0.3)[0]


def after(values, *others):
    return lax.optimization_barrier((values, others))[0]


def corr_kernel(scale, left, left_edge, right, right_edge, b4, b2, core, disp, start, table,
                mot3, mot_edge, wide):
    rows = right.shape[0]
    group = 8
    odd = lax.rem(lax.axis_index("cols"), 2)
    scale = scale[...]
    lane = lax.broadcasted_iota(jnp.int32, (24, 128), 1)
    keep = (jnp.where(lane < 72, ~7, ~3), jnp.where(lane < 18, ~1, ~0))
    last_lane = lax.broadcasted_iota(jnp.int32, (8, 128), 1) == 127

    def body(g, carry):
        scores, places = [], ([], [])
        for k in range(group):
            h = g * group + k
            window = jnp.concatenate(
                [b4[h], core[1 - odd, h], b2[h], core[odd, h], right[h], right_edge[h]], axis=0)
            pixels = jnp.concatenate([left[h], left_edge[h]], axis=0)
            s = lax.dot_general(pixels, window, (((1,), (1,)), ((), ())), preferred_element_type=jnp.float32)
            s = jnp.concatenate([s, jnp.zeros((s.shape[0], 128 - s.shape[1]), jnp.float32)], axis=1)
            ends = jnp.where(last_lane, pltpu.roll(s[16:], 32, 1), s[16:])
            scores.append(s[:16] * scale[:16])
            scores.append(ends * scale[16:])
            d = disp[h]
            for n in range(2):
                places[n].append((start[n] - (d & keep[n])) & 127)
        c = jnp.concatenate(scores, axis=0)
        found = [jnp.take_along_axis(c, jnp.concatenate(p, axis=0), axis=1, mode="promise_in_bounds") for p in places]
        motion = jnp.maximum(dot(jnp.concatenate(found, axis=1).astype(jnp.bfloat16), table[...]), 0.0)
        for k in range(group):
            h = g * group + k
            m = motion[24 * k: 24 * k + 24]
            wide[pl.ds(32 * k + 8, 16), :] = m[:16]
            mot_edge[h] = m[16:]
            wide[pl.ds(32 * k + 7, 1), :] = m[18:19]
            wide[pl.ds(32 * k + 24, 1), :] = m[19:20]
        for k in range(group):
            h = g * group + k
            mot3[h] = jnp.concatenate(
                [wide[pl.ds(32 * k + 7 + b, 16), :].astype(jnp.bfloat16) for b in range(3)], axis=1)
        return carry

    lax.fori_loop(0, rows // group, body, 0)


def motion_chunk(i, k, scale, left, left_edge, right, right_edge, b4, b2, core, disp, start, table):
    rows = b4.shape[0]
    hid = table.shape[1]

    def kernel(scale, left, left_edge, right, right_edge, b4, b2, core, disp, *rest):
        here = pl.ds(k * rows, rows)
        corr_kernel(scale.at[i], left.at[i, here], left_edge.at[i, here], right, right_edge.at[i, here],
                    b4, b2, core, disp.at[i, here], *rest)

    return call(kernel, "motion", [((rows, 16, 3 * hid), jnp.bfloat16), ((rows, 8, hid), jnp.float32)],
                [pltpu.VMEM((8 * 32, hid), jnp.float32)],
                (scale, left, left_edge, right, right_edge, b4, b2, core, disp, start, table), 2.7)


def gru_kernel(count, hid3, state, hid_edge, *refs):
    mots, edges = refs[:count], refs[count:2 * count]
    (up_z, up_r, up_q, up_edge, gates, cand, out, mot, mot_edge, z_keep, wide, res3) = refs[2 * count:]
    rows = state.shape[0]
    hid = state.shape[-1]
    each = rows // count
    zero = jnp.zeros((1, 16, 3 * hid), jnp.bfloat16)
    mot[0:1] = zero
    mot[rows + 1: rows + 2] = zero
    res3[0:1] = zero
    res3[rows + 1: rows + 2] = zero
    mot_edge[0:8] = jnp.zeros((8, hid), jnp.float32)
    mot_edge[8 * (rows + 1): 8 * (rows + 2)] = jnp.zeros((8, hid), jnp.float32)
    for k in range(count):
        mot[1 + each * k: 1 + each * (k + 1)] = mots[k][...]
        mot_edge[8 + 8 * each * k: 8 + 8 * each * (k + 1)] = edges[k][...].reshape(8 * each, hid)
    block = 16

    acc = up_edge[...]
    for a in range(3):
        for b in range(3):
            pieces = [
                jnp.concatenate([src[pl.ds(8 * a + 2 * b + side, rows, stride=8), :] for side in range(2)], axis=0)
                for src in (hid_edge, mot_edge)]
            acc += dot(jnp.concatenate(pieces, axis=1).astype(jnp.bfloat16),
                       gates[3 * a + b, 0: 2 * hid, hid: 2 * hid])
    centre = jnp.concatenate([hid_edge[pl.ds(8 + 2 + side, rows, stride=8), :] for side in range(2)], axis=0)
    reset = jax.nn.sigmoid(acc) * centre
    wide[pl.ds(7, rows, stride=32), :] = reset[:rows]
    wide[pl.ds(24, rows, stride=32), :] = reset[rows:]

    def taps(first, weights, source, r0, start):
        acc = start
        for a in range(3):
            one = source[pl.ds(r0 + a, block)].reshape(block * 16, 3 * hid)
            two = mot[pl.ds(r0 + a, block)].reshape(block * 16, 3 * hid)
            for b in range(3):
                lhs = jnp.concatenate([one[:, b * hid:(b + 1) * hid], two[:, b * hid:(b + 1) * hid]], axis=1)
                acc += dot(lhs, weights[3 * a + b, 0: 2 * hid, :])
        return acc

    def upsampled(g, *refs):
        parts = []
        for cell in range(block // 8):
            kinds = [jnp.concatenate([ref[g * (block // 8) + cell, kind] for ref in refs], axis=1) for kind in range(3)]
            parts += [kinds[0]] + [kinds[1]] * 6 + [kinds[2]]
        return jnp.concatenate(parts, axis=0)

    def gate_body(g, carry):
        r0 = g * block
        acc = taps(0, gates, hid3, r0, upsampled(g, up_z, up_r))
        both = jax.nn.sigmoid(acc)
        h = state[pl.ds(r0, block)].reshape(block * 16, hid).astype(jnp.float32)
        z_keep[pl.ds(r0 * 16, block * 16), :] = both[:, :hid]
        reset = both[:, hid:] * h
        for k in range(block):
            wide[pl.ds(pl.multiple_of((r0 + k) * 32, 32) + 8, 16), :] = reset[16 * k: 16 * k + 16]
        for k in range(block):
            res3[r0 + k + 1] = jnp.concatenate(
                [wide[pl.ds(pl.multiple_of((r0 + k) * 32, 32) + 7 + b, 16), :].astype(jnp.bfloat16)
                 for b in range(3)], axis=1)
        return carry

    lax.fori_loop(0, rows // block, gate_body, 0)

    def cand_body(g, carry):
        r0 = g * block
        q = jnp.tanh(taps(0, cand, res3, r0, upsampled(g, up_q)))
        h = state[pl.ds(r0, block)].reshape(block * 16, hid).astype(jnp.float32)
        z = z_keep[pl.ds(r0 * 16, block * 16), :]
        new = (1.0 - z) * h + z * q
        out[pl.ds(r0, block)] = new.astype(jnp.bfloat16).reshape(block, 16, hid)
        return carry

    lax.fori_loop(0, rows // block, cand_body, 0)


def fine_gru(i, before, hid3, state, hid_edge, mots, edges, ups, up_edge, gates, cand):
    images, rows, cols, hid = state.shape
    count = len(mots)
    vmem = pl.BlockSpec(memory_space=pltpu.VMEM)
    tall = rows // 8

    def kernel(hid3, state, hid_edge, *refs):
        refs = list(refs)
        if before is not None:
            refs = refs[1:]
        for n in range(3):
            refs[2 * count + n] = refs[2 * count + n].at[pl.ds(tall * i, tall)]
        refs[2 * count + 3] = refs[2 * count + 3].at[i]
        gru_kernel(count, hid3.at[i], state.at[i], hid_edge.at[i], *refs)

    args = [hid3, state, hid_edge]
    rest = [*mots, *edges, *(u.reshape(-1, 3, 16, hid) for u in ups), up_edge, gates, cand]
    first = [] if before is None else [before]
    return pl.pallas_call(
        kernel,
        grid=(1,),
        out_shape=jax.ShapeDtypeStruct(state.shape, jnp.bfloat16),
        in_specs=[vmem] * 3 + [pl.BlockSpec(memory_space=pl.ANY)] * len(first) + [vmem] * len(rest),
        out_specs=pl.BlockSpec((None, rows, cols, hid), lambda _: (i, 0, 0, 0)),
        input_output_aliases={3: 0} if first else {},
        compiler_params=pltpu.CompilerParams(vmem_limit_bytes=16 << 20),
        scratch_shapes=[pltpu.VMEM((rows + 2, 16, 3 * hid), jnp.bfloat16),
                        pltpu.VMEM((8 * (rows + 2), hid), jnp.float32),
                        pltpu.VMEM((rows * 16, hid), jnp.float32),
                        pltpu.VMEM((rows * 32, hid), jnp.float32),
                        pltpu.VMEM((rows + 2, 16, 3 * hid), jnp.bfloat16)],
        name="fine_gru",
        cost_estimate=cost(5),
    )(*(near(v) for v in args), *first, *(near(v) for v in rest))


def lookup_places():
    level = np.full((2, 128), -1)
    offset = np.zeros((2, 128), np.int64)
    for group, first, k in ((0, 0, 3), (0, 72, 2), (1, 0, 1), (1, 18, 0)):
        count = (2 * RADIUS + 1) << k
        level[group, first: first + count] = k
        offset[group, first: first + count] = ((RADIUS + 1) << k) - 1 - np.arange(count)
    tap = np.where(level >= 0, (offset >> np.maximum(level, 0)) + RADIUS, 0)
    return level, offset, tap


def lookup_pick(channels):
    level, _, tap = (v.reshape(-1) for v in lookup_places())
    rows = np.maximum(level, 0) * (2 * RADIUS + 1) + tap
    pick = np.zeros((level.size, channels), np.float32)
    pick[np.arange(level.size), rows] = np.where(level >= 0, 0.5 ** np.maximum(level, 0), 0.0)
    return jnp.asarray(pick.astype(jnp.bfloat16))


def local(left_feat, right_feat, bounds, disparity, hidden_fine, hidden_coarse, motion_weight,
          fine_gates, fine_candidate, coarse_gates, coarse_candidate):
    images, rows, cols, channels = left_feat.shape
    hid = hidden_fine.shape[-1]
    many = images * rows
    each = rows // CHUNKS
    keys = [(i, k) for i in range(images) for k in range(CHUNKS)]
    bf16, f32 = jnp.bfloat16, jnp.float32

    own = [right_feat[i, k * each:(k + 1) * each] for i, k in keys]

    disp = disparity.reshape(many, cols)
    cells = hidden_coarse.shape[1] * hidden_coarse.shape[2] * images
    to_next, to_prev, to_far, flat = call(
        functools.partial(pack_kernel, len(own)), "pack",
        [((3 * many + cells + 16, channels), bf16), ((5 * many + cells + 16, channels), bf16), ((many, channels), bf16),
         ((cells, channels), bf16)],
        [pltpu.VMEM((cells, hid), f32)],
        (left_feat, *own, hidden_fine, hidden_coarse.reshape(-1, hid), disp), 1)
    prev = permute(to_next, lambda j: j + 1)
    foll = permute(to_prev, lambda j: j - 1)
    far = permute(to_far, lambda j: j + 5)
    behind2 = permute(flat, lambda j: j + 2)
    ahead2 = permute(flat, lambda j: j - 2)
    own, prev, foll, far, behind2, ahead2 = lax.optimization_barrier((own, prev, foll, far, behind2, ahead2))
    b4 = [permute(value, lambda j: j + 4) for value in own]
    chosen, b2, core = [], [], []

    def along_y(n, *others):
        chosen.append(choose(own[n], after(b4[n], *others)))
        b2.append(permute(chosen[n], lambda j: j ^ 2))

    def joined(n, *others):
        both = join(after(b2[n], *others), own[n], b4[n])
        core.append(permute(both, lambda j: j ^ 1))
        return both

    where_x = np.array(list(range(cols)) + list(EDGE), np.int32)[:, None]
    lane = np.arange(128, dtype=np.int32)[None]
    column_of = np.where(lane == 127, -65, np.where(lane < 82, lane - 64, 1000))
    distance = where_x - column_of
    distance = jnp.asarray(np.where((distance >= 0) & (distance < MAXD), distance, -1).astype(np.int32))
    _, offset, _ = lookup_places()
    start = jnp.asarray((where_x + 64 - offset[:, None, :]).astype(np.int32))
    pick = lookup_pick(motion_weight.shape[0])

    left_edge, right_edge, disp24, hid_edge, hid3, table, scale = call(
        edge_kernel, "edges",
        [((images, rows, 8, channels), bf16), ((images, rows, 16, channels), bf16), ((images, rows, 24, 128), jnp.int32),
         ((images, 8 * (rows + 2), hid), f32), ((images, rows + 2, cols, 3 * hid), bf16), ((pick.shape[0], hid), bf16),
         ((images, 24, 128), f32)],
        [pltpu.VMEM((16 * 32, hid), f32)],
        (bounds, prev, foll, far, to_next, to_prev, hidden_fine, disp, pick, motion_weight, distance), 2, smem=1)
    new, *ups, up_edge = call(
        coarse_kernel, "coarse",
        [((cells, hid), bf16)] + [((cells // 2 * 48, hid), f32)] * 3 + [((images, 2 * rows, hid), f32)],
        [pltpu.VMEM((2, 5 * cells, hid), f32), pltpu.VMEM((3, 4 * cells, 2 * hid), bf16), pltpu.VMEM((cells, hid), f32)],
        (behind2, prev, flat, foll, ahead2, coarse_gates, coarse_candidate, fine_gates, fine_candidate), 1.5)
    coarse_new = new.reshape(hidden_coarse.shape)

    motions = []

    def motion(n, *others):
        i, k = keys[n]
        motions.append(motion_chunk(i, k, scale, left_feat, left_edge, own[n], right_edge, b4[n], b2[n],
                                    after(core[n], *others), disp24, start, table))
        return motions[n]

    def fine(i, before, *others):
        mine = [m for m, key in zip(motions, keys) if key[0] == i]
        return fine_gru(i, before, after(hid3, *others), hidden_fine, hid_edge, [m for m, _ in mine], [e for _, e in mine],
                        ups, up_edge, fine_gates, fine_candidate)

    along_y(0, table, new)
    along_y(1)
    along_y(2)
    along_y(3)
    for n in range(4):
        joined(n)
    for n in range(4):
        motion(n)
    result = fine(0, None)
    return (fine(1, result), coarse_new)


def solution(mesh):
    return jax.shard_map(
        local,
        mesh=mesh,
        in_specs=(
            P("groups", None, "cols", None),
            P("groups", None, "cols", None),
            P("groups"),
            P("groups", None, "cols"),
            P("groups", None, "cols", None),
            P("groups", None, "cols", None),
            P(),
            P(),
            P(),
            P(),
            P(),
        ),
        out_specs=(P("groups", None, "cols", None), P("groups", None, "cols", None)),
        check_vma=False,
    )
```

```python
import functools

import jax
import jax.numpy as jnp
import numpy as np
from jax import lax
from jax.experimental import pallas as pl
from jax.experimental.pallas import tpu as pltpu
from jax.sharding import PartitionSpec as P

LEVELS = 4
RADIUS = 4
MAXD = 64
CHUNKS = 2
EDGE = (-2, 15, -1, 16, 0, 17, 0, 0)


def permute(value, target, take=lambda j: True):
    count = lax.axis_size("cols")
    pairs = [(j, target(j) % count) for j in range(count) if take(j)]
    return lax.ppermute(value, "cols", pairs)


def near(value):
    return pltpu.with_memory_space_constraint(value, pltpu.VMEM)


def dot(a, b):
    return jnp.dot(a, b, preferred_element_type=jnp.float32)


def onehot(shape, column):
    r = lax.broadcasted_iota(jnp.int32, shape, 0)
    c = lax.broadcasted_iota(jnp.int32, shape, 1)
    return jnp.where(column(r, c), 1.0, 0.0).astype(jnp.bfloat16)


def cost(us):
    return pl.CostEstimate(flops=0, bytes_accessed=int(us * 3.5e6), transcendentals=0)


def call(kernel, name, outs, scratch, args, us, limit=8, smem=0, **kw):
    vmem = pl.BlockSpec(memory_space=pltpu.VMEM)
    return pl.pallas_call(
        kernel,
        out_shape=tuple(pltpu.VMEM(shape, dtype) for shape, dtype in outs),
        in_specs=[pl.BlockSpec(memory_space=pltpu.SMEM)] * smem + [vmem] * (len(args) - smem),
        out_specs=(vmem,) * len(outs),
        scratch_shapes=scratch,
        compiler_params=pltpu.CompilerParams(vmem_limit_bytes=limit << 20),
        name=name,
        cost_estimate=cost(us),
        **kw,
    )(*args[:smem], *(near(a) for a in args[smem:]))


def pack_kernel(count, left, *refs):
    rights = refs[:count]
    state, coarse, disp, to_next, to_prev, far, flat, pooled = refs[count:]
    images, rows, cols, channels = left.shape
    hid = state.shape[-1]
    many = images * rows
    wide = 16 * cols
    each = many // count

    def end(q):
        return q + jnp.where(q >= 2, cols - 4, 0)

    ends = onehot((64, wide), lambda r, c: c == (r & 15) * cols + end(r >> 4))
    per_cell = onehot((8, wide), lambda r, c: (r == (c // (8 * cols)) * (cols // 8) + (c % cols) // 8))
    for b in range(many // 16):
        i, r0 = divmod(16 * b, rows)
        here = pl.ds(16 * b, 16)

        def put(ref, slot, value):
            ref[pl.ds(many * slot + 16 * b, 16), :] = value.astype(jnp.bfloat16)

        e = dot(ends, left[i, r0: r0 + 16].reshape(wide, channels))
        put(to_prev, 0, e[:16])
        put(to_prev, 1, e[16:32])
        put(to_next, 0, e[32:48])
        put(to_next, 1, e[48:])
        e = dot(ends, rights[16 * b // each][16 * b % each: 16 * b % each + 16].reshape(wide, channels))
        put(to_prev, 2, e[:16])
        put(to_prev, 3, e[16:32])
        put(far, 0, e[48:])
        fine = state[i, r0: r0 + 16].reshape(wide, hid)
        e = dot(ends, fine)
        put(to_prev, 4, jnp.concatenate([e[:16], e[16:32]], axis=1))
        put(to_next, 2, jnp.concatenate([e[32:48], e[48:]], axis=1))
        cells = 2 * (cols // 8)
        pooled[pl.ds(cells * b, cells), :] = (dot(per_cell, fine) * (1.0 / 64))[:cells]
    both = jnp.concatenate([coarse[...], pooled[...].astype(jnp.bfloat16)], axis=1)
    flat[...] = both
    to_next[pl.ds(3 * many, flat.shape[0]), :] = both
    to_prev[pl.ds(5 * many, flat.shape[0]), :] = both
    pick = onehot((16, cols), lambda r, c: (c == end(r)) & (r < 4))
    d = lax.dot_general(pick, disp[...].astype(jnp.float32).astype(jnp.bfloat16), (((1,), (1,)), ((), ())),
                        preferred_element_type=jnp.float32)
    d = jnp.concatenate([d, jnp.zeros((16, channels - many), jnp.float32)], axis=1).astype(jnp.bfloat16)
    to_next[pl.ds(3 * many + flat.shape[0], 16), :] = d
    to_prev[pl.ds(5 * many + flat.shape[0], 16), :] = d


def edge_kernel(bounds, prev, foll, far, to_next, to_prev, state, disp, pick, motion_weight, distance, left_edge, right_edge, disp24, hid_edge,
                hid3, table, scale, wide):
    table[...] = dot(pick[...], motion_weight[...]).astype(jnp.bfloat16)
    images, rows, cols, hid = state.shape
    many = images * rows
    channels = prev.shape[1]
    for i in range(images):
        known = (distance[...] >= 0) & (distance[...] < bounds[i])
        scale[i] = jnp.where(known, jnp.float32(channels ** -0.5), 0.0)
    last = prev.shape[0] - 16
    spread8 = onehot((128, 96), lambda r, c: c == (r & 7) * 16 + (r >> 3))
    spread16 = onehot((256, 48), lambda r, c: c == jnp.where((r & 15) == 15, 2, jnp.where((r & 15) < 2, r & 15, 9)) * 16 + (r >> 4))

    own = disp[...].astype(jnp.float32).astype(jnp.bfloat16)
    d24 = dot(own, onehot((cols, cols + 8), lambda r, c: (r == c) | ((c == cols + 1) & (r == cols - 1))
                          | ((c == cols + 4) & (r == 0))))
    for ref, first, slots in ((prev, last, ((2, 0), (3, 2))), (foll, foll.shape[0] - 16, ((0, 3), (1, 5)))):
        rows16 = ref[pl.ds(first, 16), :many]
        place = onehot((16, cols + 8), lambda r, c: ((r == slots[0][0]) & (c == cols + slots[0][1]))
                       | ((r == slots[1][0]) & (c == cols + slots[1][1])))
        d24 += lax.dot_general(rows16, place, (((0,), (0,)), ((), ())), preferred_element_type=jnp.float32)
    d24 = d24.astype(jnp.bfloat16)
    slots = cols + 8
    repeat = onehot((16 * slots, 16), lambda r, c: c == r // slots)
    match = lax.broadcasted_iota(jnp.int32, (16 * slots, slots), 0) % slots \
        == lax.broadcasted_iota(jnp.int32, (16 * slots, slots), 1)
    ones = jnp.ones((slots, 128), jnp.bfloat16)

    for i in range(images):
        for line in (0, rows + 1):
            hid3[i, line] = jnp.zeros((cols, 3 * hid), jnp.bfloat16)
            hid_edge[i, pl.ds(8 * line, 8), :] = jnp.zeros((8, hid), jnp.float32)
    for b in range(many // 16):
        i, r0 = divmod(16 * b, rows)

        def get(ref, slot):
            return ref[pl.ds(many * slot + 16 * b, 16), :]

        e = dot(spread8, jnp.concatenate([get(prev, 0), get(to_next, 1), get(prev, 1), get(foll, 0), get(to_prev, 0),
                                          get(foll, 1)], axis=0))
        left_edge[i, r0: r0 + 16] = e.reshape(16, 8, channels).astype(jnp.bfloat16)
        e = dot(spread16, jnp.concatenate([get(foll, 2), get(foll, 3), get(far, 0)], axis=0))
        right_edge[i, r0: r0 + 16] = e.reshape(16, 16, channels).astype(jnp.bfloat16)
        hp, hn, on, op = get(prev, 2), get(foll, 4), get(to_next, 2), get(to_prev, 4)
        e = dot(spread8, jnp.concatenate([hp[:, :hid], on[:, hid:], hp[:, hid:], hn[:, :hid], op[:, :hid], hn[:, hid:]],
                                         axis=0))
        hid_edge[i, pl.ds(8 + 8 * r0, 128), :] = e
        for k in range(16):
            wide[pl.ds(32 * k + 8, cols), :] = state[i, r0 + k].astype(jnp.float32)
        wide[pl.ds(7, 16, stride=32), :] = hp[:, hid:].astype(jnp.float32)
        wide[pl.ds(8 + cols, 16, stride=32), :] = hn[:, :hid].astype(jnp.float32)
        for k in range(16):
            hid3[i, 1 + r0 + k] = jnp.concatenate(
                [wide[pl.ds(32 * k + 7 + t, cols), :].astype(jnp.bfloat16) for t in range(3)], axis=1)
        spread = jnp.where(match, dot(repeat, d24[16 * b: 16 * b + 16]), 0.0).astype(jnp.bfloat16)
        disp24[i, r0: r0 + 16] = dot(spread, ones).astype(jnp.int32).reshape(16, slots, 128)


def coarse_kernel(behind2, prev, flat, foll, ahead2, gates, cand, fine_gates, fine_cand, new, up_z, up_r, up_q, up_edge,
                  columns, shifted, scratch):
    count = flat.shape[0]
    cells = count // 2
    hid = new.shape[1]
    images = up_edge.shape[0]
    tall = cells // images

    def moved(value, by):
        row = lax.broadcasted_iota(jnp.int32, value.shape, 0) % tall
        if by > 0:
            return jnp.where(row == 0, 0.0, pltpu.roll(value, 1, 0))
        return jnp.where(row == tall - 1, 0.0, pltpu.roll(value, value.shape[0] - 1, 0))

    many3, many5 = prev.shape[0] - 16 - count, foll.shape[0] - 16 - count
    sources = (behind2[...], prev[pl.ds(many3, count), :], flat[...], foll[pl.ds(many5, count), :], ahead2[...])
    for n, source in enumerate(sources):
        for half in range(2):
            columns[half, pl.ds(count * n, count), :] = source[:, half * hid:(half + 1) * hid].astype(jnp.float32)
    state = []
    for n in range(8):
        parts = [columns[half, pl.ds(count * ((n + 1) // 2) + (n + 1) % 2, cells, stride=2), :] for half in range(2)]
        state.append(parts[0])
        both = jnp.concatenate(parts, axis=1)
        for a in range(3):
            value = both if a == 1 else moved(both, 1 - a)
            shifted[a, pl.ds(cells * n, cells), :] = value.astype(jnp.bfloat16)
    acc = jnp.zeros((6 * cells, 2 * hid), jnp.float32)
    for a in range(3):
        for b in range(3):
            acc += dot(shifted[a, pl.ds(cells * b, 6 * cells), :], gates[3 * a + b])
    zr = jax.nn.sigmoid(acc)
    reset = zr[:, hid:] * jnp.concatenate(state[1:7], axis=0)
    reset = reset.astype(jnp.bfloat16).astype(jnp.float32)
    acc = jnp.zeros((4 * cells, hid), jnp.float32)
    for a in range(3):
        value = (reset if a == 1 else moved(reset, 1 - a)).astype(jnp.bfloat16)
        for b in range(3):
            lhs = jnp.concatenate([value[cells * b: cells * (b + 4)],
                                   shifted[a, pl.ds(cells * (b + 1), 4 * cells), hid:]], axis=1)
            acc += dot(lhs, cand[3 * a + b])
    q = jnp.tanh(acc)
    z = zr[cells: 5 * cells, :hid]
    fresh = (1.0 - z) * jnp.concatenate(state[2:6], axis=0) + z * q
    rounded = fresh.astype(jnp.bfloat16)
    for n in range(2):
        scratch[pl.ds(n, cells, stride=2), :] = fresh[cells * (n + 1): cells * (n + 2)]
    new[...] = scratch[...].astype(jnp.bfloat16)

    sums = []
    for b in range(3):
        p = []
        for a in range(3):
            w = jnp.concatenate([fine_gates[3 * a + b, 2 * hid:, :], fine_cand[3 * a + b, 2 * hid:, :]], axis=1)
            p.append(dot(rounded, w))
        low = p[0] + p[1]
        sums.append((moved(p[0], 1) + p[1] + p[2], low + p[2], low + moved(p[2], -1)))

    def at(kind, js):
        return sum(sums[b][kind][cells * (js[b] + 1): cells * (js[b] + 2)] for b in range(3))

    for kind in range(3):
        inner = {0: (-1, 0, 0), 7: (0, 0, 1), 8: (0, 1, 1), 15: (1, 1, 2)}
        flat0, flat1 = at(kind, (0, 0, 0)), at(kind, (1, 1, 1))
        for x in range(16):
            value = at(kind, inner[x]) if x in inner else (flat0 if x < 8 else flat1)
            for part, ref in enumerate((up_z, up_r, up_q)):
                ref[pl.ds(kind * 16 + x, cells, stride=48), :] = value[:, part * hid:(part + 1) * hid]
        for side, js in enumerate(((-1, -1, 0), (1, 2, 2))):
            value = at(kind, js)[:, hid: 2 * hid]
            for i in range(images):
                for u in ((0,), range(1, 7), (7,))[kind]:
                    up_edge[i, pl.ds(side * 8 * tall + u, tall, stride=8), :] = value[tall * i: tall * (i + 1)]


def copy_either(second_wanted, first, second, out):
    @pl.when(jnp.logical_not(second_wanted))
    def _():
        out[...] = first[...]

    @pl.when(second_wanted)
    def _():
        out[...] = second[...]


def choose_kernel(mine, came, out):
    copy_either(lax.rem(lax.axis_index("cols"), 4) >= 2, mine, came, out)


def choose(mine, came):
    return call(choose_kernel, "choose", [(mine.shape, mine.dtype)], [], (mine, came), 0.2)[0]


def join_kernel(second, mine, came, out):
    out[0] = second[...]
    copy_either(lax.rem(lax.axis_index("cols"), 2) == 1, mine, came, out.at[1])


def join(second, mine, came):
    return call(join_kernel, "join", [((2,) + mine.shape, mine.dtype)], [], (second, mine, came), 0.3)[0]


def after(values, *others):
    return lax.optimization_barrier((values, others))[0]


def corr_kernel(scale, left, left_edge, right, right_edge, b4, b2, core, disp, start, table,
                mot3, mot_edge, wide):
    rows = right.shape[0]
    group = 8
    odd = lax.rem(lax.axis_index("cols"), 2)
    scale = scale[...]
    lane = lax.broadcasted_iota(jnp.int32, (24, 128), 1)
    keep = (jnp.where(lane < 72, ~7, ~3), jnp.where(lane < 18, ~1, ~0))
    last_lane = lax.broadcasted_iota(jnp.int32, (8, 128), 1) == 127

    def body(g, carry):
        scores, places = [], ([], [])
        for k in range(group):
            h = g * group + k
            window = jnp.concatenate(
                [b4[h], core[1 - odd, h], b2[h], core[odd, h], right[h], right_edge[h]], axis=0)
            pixels = jnp.concatenate([left[h], left_edge[h]], axis=0)
            s = lax.dot_general(pixels, window, (((1,), (1,)), ((), ())), preferred_element_type=jnp.float32)
            s = jnp.concatenate([s, jnp.zeros((s.shape[0], 128 - s.shape[1]), jnp.float32)], axis=1)
            ends = jnp.where(last_lane, pltpu.roll(s[16:], 32, 1), s[16:])
            scores.append(s[:16] * scale[:16])
            scores.append(ends * scale[16:])
            d = disp[h]
            for n in range(2):
                places[n].append((start[n] - (d & keep[n])) & 127)
        c = jnp.concatenate(scores, axis=0)
        found = [jnp.take_along_axis(c, jnp.concatenate(p, axis=0), axis=1, mode="promise_in_bounds") for p in places]
        motion = jnp.maximum(dot(jnp.concatenate(found, axis=1).astype(jnp.bfloat16), table[...]), 0.0)
        for k in range(group):
            h = g * group + k
            m = motion[24 * k: 24 * k + 24]
            wide[pl.ds(32 * k + 8, 16), :] = m[:16]
            mot_edge[h] = m[16:]
            wide[pl.ds(32 * k + 7, 1), :] = m[18:19]
            wide[pl.ds(32 * k + 24, 1), :] = m[19:20]
        for k in range(group):
            h = g * group + k
            mot3[h] = jnp.concatenate(
                [wide[pl.ds(32 * k + 7 + b, 16), :].astype(jnp.bfloat16) for b in range(3)], axis=1)
        return carry

    lax.fori_loop(0, rows // group, body, 0)


def motion_chunk(i, k, scale, left, left_edge, right, right_edge, b4, b2, core, disp, start, table):
    rows = b4.shape[0]
    hid = table.shape[1]

    def kernel(scale, left, left_edge, right, right_edge, b4, b2, core, disp, *rest):
        here = pl.ds(k * rows, rows)
        corr_kernel(scale.at[i], left.at[i, here], left_edge.at[i, here], right, right_edge.at[i, here],
                    b4, b2, core, disp.at[i, here], *rest)

    return call(kernel, "motion", [((rows, 16, 3 * hid), jnp.bfloat16), ((rows, 8, hid), jnp.float32)],
                [pltpu.VMEM((8 * 32, hid), jnp.float32)],
                (scale, left, left_edge, right, right_edge, b4, b2, core, disp, start, table), 2.7)


def gru_kernel(count, hid3, state, hid_edge, *refs):
    mots, edges = refs[:count], refs[count:2 * count]
    (up_z, up_r, up_q, up_edge, gates, cand, out, mot, mot_edge, z_keep, wide, res3) = refs[2 * count:]
    rows = state.shape[0]
    hid = state.shape[-1]
    each = rows // count
    zero = jnp.zeros((1, 16, 3 * hid), jnp.bfloat16)
    mot[0:1] = zero
    mot[rows + 1: rows + 2] = zero
    res3[0:1] = zero
    res3[rows + 1: rows + 2] = zero
    mot_edge[0:8] = jnp.zeros((8, hid), jnp.float32)
    mot_edge[8 * (rows + 1): 8 * (rows + 2)] = jnp.zeros((8, hid), jnp.float32)
    for k in range(count):
        mot[1 + each * k: 1 + each * (k + 1)] = mots[k][...]
        mot_edge[8 + 8 * each * k: 8 + 8 * each * (k + 1)] = edges[k][...].reshape(8 * each, hid)
    block = 32

    pieces = []
    for a in range(3):
        for b in range(3):
            pieces += [
                jnp.concatenate([src[pl.ds(8 * a + 2 * b + side, rows, stride=8), :] for side in range(2)], axis=0)
                .astype(jnp.bfloat16) for src in (hid_edge, mot_edge)]
    weights = jnp.concatenate([gates[t, 0: 2 * hid, hid: 2 * hid] for t in range(9)], axis=0)
    acc = dot(jnp.concatenate(pieces, axis=1), weights) + up_edge[...]
    centre = jnp.concatenate([hid_edge[pl.ds(8 + 2 + side, rows, stride=8), :] for side in range(2)], axis=0)
    reset = jax.nn.sigmoid(acc) * centre
    wide[pl.ds(7, rows, stride=32), :] = reset[:rows]
    wide[pl.ds(24, rows, stride=32), :] = reset[rows:]

    def taps(weights, source, r0):
        pieces = []
        for a in range(3):
            one = source[pl.ds(r0 + a, block)].reshape(block * 16, 3 * hid)
            two = mot[pl.ds(r0 + a, block)].reshape(block * 16, 3 * hid)
            for b in range(3):
                pieces += [one[:, b * hid:(b + 1) * hid], two[:, b * hid:(b + 1) * hid]]
        return dot(jnp.concatenate(pieces, axis=1), jnp.concatenate([weights[t, 0: 2 * hid, :] for t in range(9)], axis=0))

    def upsampled(g, *refs):
        parts = []
        for cell in range(block // 8):
            kinds = [jnp.concatenate([ref[g * (block // 8) + cell, kind] for ref in refs], axis=1) for kind in range(3)]
            parts += [kinds[0]] + [kinds[1]] * 6 + [kinds[2]]
        return jnp.concatenate(parts, axis=0)

    def gate_body(g, carry):
        r0 = g * block
        acc = taps(gates, hid3, r0) + upsampled(g, up_z, up_r)
        both = jax.nn.sigmoid(acc)
        h = state[pl.ds(r0, block)].reshape(block * 16, hid).astype(jnp.float32)
        z_keep[pl.ds(r0 * 16, block * 16), :] = both[:, :hid]
        reset = both[:, hid:] * h
        for k in range(block):
            wide[pl.ds(pl.multiple_of((r0 + k) * 32, 32) + 8, 16), :] = reset[16 * k: 16 * k + 16]
        for k in range(block):
            res3[r0 + k + 1] = jnp.concatenate(
                [wide[pl.ds(pl.multiple_of((r0 + k) * 32, 32) + 7 + b, 16), :].astype(jnp.bfloat16)
                 for b in range(3)], axis=1)
        return carry

    lax.fori_loop(0, rows // block, gate_body, 0)

    def cand_body(g, carry):
        r0 = g * block
        q = jnp.tanh(taps(cand, res3, r0) + upsampled(g, up_q))
        h = state[pl.ds(r0, block)].reshape(block * 16, hid).astype(jnp.float32)
        z = z_keep[pl.ds(r0 * 16, block * 16), :]
        new = (1.0 - z) * h + z * q
        out[pl.ds(r0, block)] = new.astype(jnp.bfloat16).reshape(block, 16, hid)
        return carry

    lax.fori_loop(0, rows // block, cand_body, 0)


def fine_gru(i, before, hid3, state, hid_edge, mots, edges, ups, up_edge, gates, cand):
    images, rows, cols, hid = state.shape
    count = len(mots)
    vmem = pl.BlockSpec(memory_space=pltpu.VMEM)
    tall = rows // 8

    def kernel(hid3, state, hid_edge, *refs):
        refs = list(refs)
        if before is not None:
            refs = refs[1:]
        for n in range(3):
            refs[2 * count + n] = refs[2 * count + n].at[pl.ds(tall * i, tall)]
        refs[2 * count + 3] = refs[2 * count + 3].at[i]
        gru_kernel(count, hid3.at[i], state.at[i], hid_edge.at[i], *refs)

    args = [hid3, state, hid_edge]
    rest = [*mots, *edges, *(u.reshape(-1, 3, 16, hid) for u in ups), up_edge, gates, cand]
    first = [] if before is None else [before]
    return pl.pallas_call(
        kernel,
        grid=(1,),
        out_shape=jax.ShapeDtypeStruct(state.shape, jnp.bfloat16),
        in_specs=[vmem] * 3 + [pl.BlockSpec(memory_space=pl.ANY)] * len(first) + [vmem] * len(rest),
        out_specs=pl.BlockSpec((None, rows, cols, hid), lambda _: (i, 0, 0, 0)),
        input_output_aliases={3: 0} if first else {},
        compiler_params=pltpu.CompilerParams(vmem_limit_bytes=16 << 20),
        scratch_shapes=[pltpu.VMEM((rows + 2, 16, 3 * hid), jnp.bfloat16),
                        pltpu.VMEM((8 * (rows + 2), hid), jnp.float32),
                        pltpu.VMEM((rows * 16, hid), jnp.float32),
                        pltpu.VMEM((rows * 32, hid), jnp.float32),
                        pltpu.VMEM((rows + 2, 16, 3 * hid), jnp.bfloat16)],
        name="fine_gru",
        cost_estimate=cost(5),
    )(*(near(v) for v in args), *first, *(near(v) for v in rest))


def lookup_places():
    level = np.full((2, 128), -1)
    offset = np.zeros((2, 128), np.int64)
    for group, first, k in ((0, 0, 3), (0, 72, 2), (1, 0, 1), (1, 18, 0)):
        count = (2 * RADIUS + 1) << k
        level[group, first: first + count] = k
        offset[group, first: first + count] = ((RADIUS + 1) << k) - 1 - np.arange(count)
    tap = np.where(level >= 0, (offset >> np.maximum(level, 0)) + RADIUS, 0)
    return level, offset, tap


def lookup_pick(channels):
    level, _, tap = (v.reshape(-1) for v in lookup_places())
    rows = np.maximum(level, 0) * (2 * RADIUS + 1) + tap
    pick = np.zeros((level.size, channels), np.float32)
    pick[np.arange(level.size), rows] = np.where(level >= 0, 0.5 ** np.maximum(level, 0), 0.0)
    return jnp.asarray(pick.astype(jnp.bfloat16))


def local(left_feat, right_feat, bounds, disparity, hidden_fine, hidden_coarse, motion_weight,
          fine_gates, fine_candidate, coarse_gates, coarse_candidate):
    images, rows, cols, channels = left_feat.shape
    hid = hidden_fine.shape[-1]
    many = images * rows
    each = rows // CHUNKS
    keys = [(i, k) for i in range(images) for k in range(CHUNKS)]
    bf16, f32 = jnp.bfloat16, jnp.float32

    own = [right_feat[i, k * each:(k + 1) * each] for i, k in keys]

    disp = disparity.reshape(many, cols)
    cells = hidden_coarse.shape[1] * hidden_coarse.shape[2] * images
    to_next, to_prev, to_far, flat = call(
        functools.partial(pack_kernel, len(own)), "pack",
        [((3 * many + cells + 16, channels), bf16), ((5 * many + cells + 16, channels), bf16), ((many, channels), bf16),
         ((cells, channels), bf16)],
        [pltpu.VMEM((cells, hid), f32)],
        (left_feat, *own, hidden_fine, hidden_coarse.reshape(-1, hid), disp), 1)
    prev = permute(to_next, lambda j: j + 1)
    foll = permute(to_prev, lambda j: j - 1)
    far = permute(to_far, lambda j: j + 5)
    behind2 = permute(flat, lambda j: j + 2)
    ahead2 = permute(flat, lambda j: j - 2)
    own, prev, foll, far, behind2, ahead2 = lax.optimization_barrier((own, prev, foll, far, behind2, ahead2))
    b4 = [permute(value, lambda j: j + 4) for value in own]
    chosen, b2, core = [], [], []

    def along_y(n, *others):
        chosen.append(choose(own[n], after(b4[n], *others)))
        b2.append(permute(chosen[n], lambda j: j ^ 2))

    def joined(n, *others):
        both = join(after(b2[n], *others), own[n], b4[n])
        core.append(permute(both, lambda j: j ^ 1))
        return both

    where_x = np.array(list(range(cols)) + list(EDGE), np.int32)[:, None]
    lane = np.arange(128, dtype=np.int32)[None]
    column_of = np.where(lane == 127, -65, np.where(lane < 82, lane - 64, 1000))
    distance = where_x - column_of
    distance = jnp.asarray(np.where((distance >= 0) & (distance < MAXD), distance, -1).astype(np.int32))
    _, offset, _ = lookup_places()
    start = jnp.asarray((where_x + 64 - offset[:, None, :]).astype(np.int32))
    pick = lookup_pick(motion_weight.shape[0])

    left_edge, right_edge, disp24, hid_edge, hid3, table, scale = call(
        edge_kernel, "edges",
        [((images, rows, 8, channels), bf16), ((images, rows, 16, channels), bf16), ((images, rows, 24, 128), jnp.int32),
         ((images, 8 * (rows + 2), hid), f32), ((images, rows + 2, cols, 3 * hid), bf16), ((pick.shape[0], hid), bf16),
         ((images, 24, 128), f32)],
        [pltpu.VMEM((16 * 32, hid), f32)],
        (bounds, prev, foll, far, to_next, to_prev, hidden_fine, disp, pick, motion_weight, distance), 2, smem=1)
    new, *ups, up_edge = call(
        coarse_kernel, "coarse",
        [((cells, hid), bf16)] + [((cells // 2 * 48, hid), f32)] * 3 + [((images, 2 * rows, hid), f32)],
        [pltpu.VMEM((2, 5 * cells, hid), f32), pltpu.VMEM((3, 4 * cells, 2 * hid), bf16), pltpu.VMEM((cells, hid), f32)],
        (behind2, prev, flat, foll, ahead2, coarse_gates, coarse_candidate, fine_gates, fine_candidate), 1.5)
    coarse_new = new.reshape(hidden_coarse.shape)

    motions = []

    def motion(n, *others):
        i, k = keys[n]
        motions.append(motion_chunk(i, k, scale, left_feat, left_edge, own[n], right_edge, b4[n], b2[n],
                                    after(core[n], *others), disp24, start, table))
        return motions[n]

    def fine(i, before, *others):
        mine = [m for m, key in zip(motions, keys) if key[0] == i]
        return fine_gru(i, before, after(hid3, *others), hidden_fine, hid_edge, [m for m, _ in mine], [e for _, e in mine],
                        ups, up_edge, fine_gates, fine_candidate)

    along_y(0, table, new)
    along_y(1)
    along_y(2)
    along_y(3)
    for n in range(4):
        joined(n)
    for n in range(4):
        motion(n)
    result = fine(0, None)
    return (fine(1, result), coarse_new)


def solution(mesh):
    return jax.shard_map(
        local,
        mesh=mesh,
        in_specs=(
            P("groups", None, "cols", None),
            P("groups", None, "cols", None),
            P("groups"),
            P("groups", None, "cols"),
            P("groups", None, "cols", None),
            P("groups", None, "cols", None),
            P(),
            P(),
            P(),
            P(),
            P(),
        ),
        out_specs=(P("groups", None, "cols", None), P("groups", None, "cols", None)),
        check_vma=False,
    )
```

```python
import functools

import jax
import jax.numpy as jnp
import numpy as np
from jax import lax
from jax.experimental import pallas as pl
from jax.experimental.pallas import tpu as pltpu
from jax.sharding import PartitionSpec as P

LEVELS = 4
RADIUS = 4
MAXD = 64
CHUNKS = 2
EDGE = (-2, 15, -1, 16, 0, 17, 0, 0)


def permute(value, target, take=lambda j: True):
    count = lax.axis_size("cols")
    pairs = [(j, target(j) % count) for j in range(count) if take(j)]
    return lax.ppermute(value, "cols", pairs)


def near(value):
    return pltpu.with_memory_space_constraint(value, pltpu.VMEM)


def dot(a, b):
    return jnp.dot(a, b, preferred_element_type=jnp.float32)


def onehot(shape, column):
    r = lax.broadcasted_iota(jnp.int32, shape, 0)
    c = lax.broadcasted_iota(jnp.int32, shape, 1)
    return jnp.where(column(r, c), 1.0, 0.0).astype(jnp.bfloat16)


def cost(us):
    return pl.CostEstimate(flops=0, bytes_accessed=int(us * 3.5e6), transcendentals=0)


def call(kernel, name, outs, scratch, args, us, limit=8, smem=0, **kw):
    vmem = pl.BlockSpec(memory_space=pltpu.VMEM)
    return pl.pallas_call(
        kernel,
        out_shape=tuple(pltpu.VMEM(shape, dtype) for shape, dtype in outs),
        in_specs=[pl.BlockSpec(memory_space=pltpu.SMEM)] * smem + [vmem] * (len(args) - smem),
        out_specs=(vmem,) * len(outs),
        scratch_shapes=scratch,
        compiler_params=pltpu.CompilerParams(vmem_limit_bytes=limit << 20),
        name=name,
        cost_estimate=cost(us),
        **kw,
    )(*args[:smem], *(near(a) for a in args[smem:]))


def pack_kernel(count, left, *refs):
    rights = refs[:count]
    state, coarse, disp, to_next, to_prev, far, flat, pooled = refs[count:]
    images, rows, cols, channels = left.shape
    hid = state.shape[-1]
    many = images * rows
    wide = 16 * cols
    each = many // count

    def end(q):
        return q + jnp.where(q >= 2, cols - 4, 0)

    ends = onehot((64, wide), lambda r, c: c == (r & 15) * cols + end(r >> 4))
    per_cell = onehot((8, wide), lambda r, c: (r == (c // (8 * cols)) * (cols // 8) + (c % cols) // 8))
    for b in range(many // 16):
        i, r0 = divmod(16 * b, rows)
        here = pl.ds(16 * b, 16)

        def put(ref, slot, value):
            ref[pl.ds(many * slot + 16 * b, 16), :] = value.astype(jnp.bfloat16)

        e = dot(ends, left[i, r0: r0 + 16].reshape(wide, channels))
        put(to_prev, 0, e[:16])
        put(to_prev, 1, e[16:32])
        put(to_next, 0, e[32:48])
        put(to_next, 1, e[48:])
        e = dot(ends, rights[16 * b // each][16 * b % each: 16 * b % each + 16].reshape(wide, channels))
        put(to_prev, 2, e[:16])
        put(to_prev, 3, e[16:32])
        put(far, 0, e[48:])
        fine = state[i, r0: r0 + 16].reshape(wide, hid)
        e = dot(ends, fine)
        put(to_prev, 4, jnp.concatenate([e[:16], e[16:32]], axis=1))
        put(to_next, 2, jnp.concatenate([e[32:48], e[48:]], axis=1))
        cells = 2 * (cols // 8)
        pooled[pl.ds(cells * b, cells), :] = (dot(per_cell, fine) * (1.0 / 64))[:cells]
    both = jnp.concatenate([coarse[...], pooled[...].astype(jnp.bfloat16)], axis=1)
    flat[...] = both
    to_next[pl.ds(3 * many, flat.shape[0]), :] = both
    to_prev[pl.ds(5 * many, flat.shape[0]), :] = both
    pick = onehot((16, cols), lambda r, c: (c == end(r)) & (r < 4))
    d = lax.dot_general(pick, disp[...].astype(jnp.float32).astype(jnp.bfloat16), (((1,), (1,)), ((), ())),
                        preferred_element_type=jnp.float32)
    d = jnp.concatenate([d, jnp.zeros((16, channels - many), jnp.float32)], axis=1).astype(jnp.bfloat16)
    to_next[pl.ds(3 * many + flat.shape[0], 16), :] = d
    to_prev[pl.ds(5 * many + flat.shape[0], 16), :] = d


def edge_kernel(bounds, prev, foll, far, to_next, to_prev, state, disp, pick, motion_weight, distance, left_edge, right_edge, disp24, hid_edge,
                hid3, table, scale, wide):
    table[...] = dot(pick[...], motion_weight[...]).astype(jnp.bfloat16)
    images, rows, cols, hid = state.shape
    many = images * rows
    channels = prev.shape[1]
    for i in range(images):
        known = (distance[...] >= 0) & (distance[...] < bounds[i])
        scale[i] = jnp.where(known, jnp.float32(channels ** -0.5), 0.0)
    last = prev.shape[0] - 16
    spread8 = onehot((128, 96), lambda r, c: c == (r & 7) * 16 + (r >> 3))
    spread16 = onehot((256, 48), lambda r, c: c == jnp.where((r & 15) == 15, 2, jnp.where((r & 15) < 2, r & 15, 9)) * 16 + (r >> 4))

    own = disp[...].astype(jnp.float32).astype(jnp.bfloat16)
    d24 = dot(own, onehot((cols, cols + 8), lambda r, c: (r == c) | ((c == cols + 1) & (r == cols - 1))
                          | ((c == cols + 4) & (r == 0))))
    for ref, first, slots in ((prev, last, ((2, 0), (3, 2))), (foll, foll.shape[0] - 16, ((0, 3), (1, 5)))):
        rows16 = ref[pl.ds(first, 16), :many]
        place = onehot((16, cols + 8), lambda r, c: ((r == slots[0][0]) & (c == cols + slots[0][1]))
                       | ((r == slots[1][0]) & (c == cols + slots[1][1])))
        d24 += lax.dot_general(rows16, place, (((0,), (0,)), ((), ())), preferred_element_type=jnp.float32)
    d24 = d24.astype(jnp.bfloat16)
    slots = cols + 8
    repeat = onehot((16 * slots, 16), lambda r, c: c == r // slots)
    match = lax.broadcasted_iota(jnp.int32, (16 * slots, slots), 0) % slots \
        == lax.broadcasted_iota(jnp.int32, (16 * slots, slots), 1)
    ones = jnp.ones((slots, 128), jnp.bfloat16)

    for i in range(images):
        for line in (0, rows + 1):
            hid3[i, line] = jnp.zeros((cols, 3 * hid), jnp.bfloat16)
            hid_edge[i, pl.ds(8 * line, 8), :] = jnp.zeros((8, hid), jnp.float32)
    for b in range(many // 16):
        i, r0 = divmod(16 * b, rows)

        def get(ref, slot):
            return ref[pl.ds(many * slot + 16 * b, 16), :]

        e = dot(spread8, jnp.concatenate([get(prev, 0), get(to_next, 1), get(prev, 1), get(foll, 0), get(to_prev, 0),
                                          get(foll, 1)], axis=0))
        left_edge[i, r0: r0 + 16] = e.reshape(16, 8, channels).astype(jnp.bfloat16)
        e = dot(spread16, jnp.concatenate([get(foll, 2), get(foll, 3), get(far, 0)], axis=0))
        right_edge[i, r0: r0 + 16] = e.reshape(16, 16, channels).astype(jnp.bfloat16)
        hp, hn, on, op = get(prev, 2), get(foll, 4), get(to_next, 2), get(to_prev, 4)
        e = dot(spread8, jnp.concatenate([hp[:, :hid], on[:, hid:], hp[:, hid:], hn[:, :hid], op[:, :hid], hn[:, hid:]],
                                         axis=0))
        hid_edge[i, pl.ds(8 + 8 * r0, 128), :] = e
        for k in range(16):
            wide[pl.ds(32 * k + 8, cols), :] = state[i, r0 + k].astype(jnp.float32)
        wide[pl.ds(7, 16, stride=32), :] = hp[:, hid:].astype(jnp.float32)
        wide[pl.ds(8 + cols, 16, stride=32), :] = hn[:, :hid].astype(jnp.float32)
        for k in range(16):
            hid3[i, 1 + r0 + k] = jnp.concatenate(
                [wide[pl.ds(32 * k + 7 + t, cols), :].astype(jnp.bfloat16) for t in range(3)], axis=1)
        spread = jnp.where(match, dot(repeat, d24[16 * b: 16 * b + 16]), 0.0).astype(jnp.bfloat16)
        disp24[i, r0: r0 + 16] = dot(spread, ones).astype(jnp.int32).reshape(16, slots, 128)


def coarse_kernel(behind2, prev, flat, foll, ahead2, gates, cand, fine_gates, fine_cand, new, up_z, up_r, up_q, up_edge,
                  columns, shifted, scratch):
    count = flat.shape[0]
    cells = count // 2
    hid = new.shape[1]
    images = up_edge.shape[0]
    tall = cells // images

    def moved(value, by):
        row = lax.broadcasted_iota(jnp.int32, value.shape, 0) % tall
        if by > 0:
            return jnp.where(row == 0, 0.0, pltpu.roll(value, 1, 0))
        return jnp.where(row == tall - 1, 0.0, pltpu.roll(value, value.shape[0] - 1, 0))

    many3, many5 = prev.shape[0] - 16 - count, foll.shape[0] - 16 - count
    sources = (behind2[...], prev[pl.ds(many3, count), :], flat[...], foll[pl.ds(many5, count), :], ahead2[...])
    for n, source in enumerate(sources):
        for half in range(2):
            columns[half, pl.ds(count * n, count), :] = source[:, half * hid:(half + 1) * hid].astype(jnp.float32)
    state = []
    for n in range(8):
        parts = [columns[half, pl.ds(count * ((n + 1) // 2) + (n + 1) % 2, cells, stride=2), :] for half in range(2)]
        state.append(parts[0])
        both = jnp.concatenate(parts, axis=1)
        for a in range(3):
            value = both if a == 1 else moved(both, 1 - a)
            shifted[a, pl.ds(cells * n, cells), :] = value.astype(jnp.bfloat16)
    acc = jnp.zeros((6 * cells, 2 * hid), jnp.float32)
    for a in range(3):
        for b in range(3):
            acc += dot(shifted[a, pl.ds(cells * b, 6 * cells), :], gates[3 * a + b])
    zr = jax.nn.sigmoid(acc)
    reset = zr[:, hid:] * jnp.concatenate(state[1:7], axis=0)
    reset = reset.astype(jnp.bfloat16).astype(jnp.float32)
    acc = jnp.zeros((4 * cells, hid), jnp.float32)
    for a in range(3):
        value = (reset if a == 1 else moved(reset, 1 - a)).astype(jnp.bfloat16)
        for b in range(3):
            lhs = jnp.concatenate([value[cells * b: cells * (b + 4)],
                                   shifted[a, pl.ds(cells * (b + 1), 4 * cells), hid:]], axis=1)
            acc += dot(lhs, cand[3 * a + b])
    q = jnp.tanh(acc)
    z = zr[cells: 5 * cells, :hid]
    fresh = (1.0 - z) * jnp.concatenate(state[2:6], axis=0) + z * q
    rounded = fresh.astype(jnp.bfloat16)
    for n in range(2):
        scratch[pl.ds(n, cells, stride=2), :] = fresh[cells * (n + 1): cells * (n + 2)]
    new[...] = scratch[...].astype(jnp.bfloat16)

    sums = []
    for b in range(3):
        p = []
        for a in range(3):
            w = jnp.concatenate([fine_gates[3 * a + b, 2 * hid:, :], fine_cand[3 * a + b, 2 * hid:, :]], axis=1)
            p.append(dot(rounded, w))
        low = p[0] + p[1]
        sums.append((moved(p[0], 1) + p[1] + p[2], low + p[2], low + moved(p[2], -1)))

    def at(kind, js):
        return sum(sums[b][kind][cells * (js[b] + 1): cells * (js[b] + 2)] for b in range(3))

    for kind in range(3):
        inner = {0: (-1, 0, 0), 7: (0, 0, 1), 8: (0, 1, 1), 15: (1, 1, 2)}
        flat0, flat1 = at(kind, (0, 0, 0)), at(kind, (1, 1, 1))
        for x in range(16):
            value = at(kind, inner[x]) if x in inner else (flat0 if x < 8 else flat1)
            for part, ref in enumerate((up_z, up_r, up_q)):
                ref[pl.ds(kind * 16 + x, cells, stride=48), :] = value[:, part * hid:(part + 1) * hid]
        for side, js in enumerate(((-1, -1, 0), (1, 2, 2))):
            value = at(kind, js)[:, hid: 2 * hid]
            for i in range(images):
                for u in ((0,), range(1, 7), (7,))[kind]:
                    up_edge[i, pl.ds(side * 8 * tall + u, tall, stride=8), :] = value[tall * i: tall * (i + 1)]


def copy_either(second_wanted, first, second, out):
    @pl.when(jnp.logical_not(second_wanted))
    def _():
        out[...] = first[...]

    @pl.when(second_wanted)
    def _():
        out[...] = second[...]


def choose_kernel(mine, came, out):
    copy_either(lax.rem(lax.axis_index("cols"), 4) >= 2, mine, came, out)


def choose(mine, came):
    return call(choose_kernel, "choose", [(mine.shape, mine.dtype)], [], (mine, came), 0.2)[0]


def join_kernel(second, mine, came, out):
    out[0] = second[...]
    copy_either(lax.rem(lax.axis_index("cols"), 2) == 1, mine, came, out.at[1])


def join(second, mine, came):
    return call(join_kernel, "join", [((2,) + mine.shape, mine.dtype)], [], (second, mine, came), 0.3)[0]


def after(values, *others):
    return lax.optimization_barrier((values, others))[0]


def corr_kernel(scale, left, left_edge, right, right_edge, b4, b2, core, disp, start, table,
                mot3, mot_edge, wide):
    rows = right.shape[0]
    group = 32
    odd = lax.rem(lax.axis_index("cols"), 2)
    scale = scale[...]
    lane = lax.broadcasted_iota(jnp.int32, (24, 128), 1)
    keep = (jnp.where(lane < 72, ~7, ~3), jnp.where(lane < 18, ~1, ~0))
    last_lane = lax.broadcasted_iota(jnp.int32, (8, 128), 1) == 127

    def body(g, carry):
        scores, places = [], ([], [])
        for k in range(group):
            h = g * group + k
            window = jnp.concatenate(
                [b4[h], core[1 - odd, h], b2[h], core[odd, h], right[h], right_edge[h]], axis=0)
            pixels = jnp.concatenate([left[h], left_edge[h]], axis=0)
            s = lax.dot_general(pixels, window, (((1,), (1,)), ((), ())), preferred_element_type=jnp.float32)
            s = jnp.concatenate([s, jnp.zeros((s.shape[0], 128 - s.shape[1]), jnp.float32)], axis=1)
            ends = jnp.where(last_lane, pltpu.roll(s[16:], 32, 1), s[16:])
            scores.append(s[:16] * scale[:16])
            scores.append(ends * scale[16:])
            d = disp[h]
            for n in range(2):
                places[n].append((start[n] - (d & keep[n])) & 127)
        c = jnp.concatenate(scores, axis=0)
        found = [jnp.take_along_axis(c, jnp.concatenate(p, axis=0), axis=1, mode="promise_in_bounds") for p in places]
        motion = jnp.maximum(dot(jnp.concatenate(found, axis=1).astype(jnp.bfloat16), table[...]), 0.0)
        for k in range(group):
            h = g * group + k
            m = motion[24 * k: 24 * k + 24]
            wide[pl.ds(32 * k + 8, 16), :] = m[:16]
            mot_edge[h] = m[16:]
            wide[pl.ds(32 * k + 7, 1), :] = m[18:19]
            wide[pl.ds(32 * k + 24, 1), :] = m[19:20]
        for k in range(group):
            h = g * group + k
            mot3[h] = jnp.concatenate(
                [wide[pl.ds(32 * k + 7 + b, 16), :].astype(jnp.bfloat16) for b in range(3)], axis=1)
        return carry

    lax.fori_loop(0, rows // group, body, 0)


def motion_chunk(i, k, scale, left, left_edge, right, right_edge, b4, b2, core, disp, start, table):
    rows = b4.shape[0]
    hid = table.shape[1]

    def kernel(scale, left, left_edge, right, right_edge, b4, b2, core, disp, *rest):
        here = pl.ds(k * rows, rows)
        corr_kernel(scale.at[i], left.at[i, here], left_edge.at[i, here], right, right_edge.at[i, here],
                    b4, b2, core, disp.at[i, here], *rest)

    return call(kernel, "motion", [((rows, 16, 3 * hid), jnp.bfloat16), ((rows, 8, hid), jnp.float32)],
                [pltpu.VMEM((32 * 32, hid), jnp.float32)],
                (scale, left, left_edge, right, right_edge, b4, b2, core, disp, start, table), 2.7)


def gru_kernel(count, hid3, state, hid_edge, *refs):
    mots, edges = refs[:count], refs[count:2 * count]
    (up_z, up_r, up_q, up_edge, gates, cand, out, mot, mot_edge, z_keep, wide, res3) = refs[2 * count:]
    rows = state.shape[0]
    hid = state.shape[-1]
    each = rows // count
    zero = jnp.zeros((1, 16, 3 * hid), jnp.bfloat16)
    mot[0:1] = zero
    mot[rows + 1: rows + 2] = zero
    res3[0:1] = zero
    res3[rows + 1: rows + 2] = zero
    mot_edge[0:8] = jnp.zeros((8, hid), jnp.float32)
    mot_edge[8 * (rows + 1): 8 * (rows + 2)] = jnp.zeros((8, hid), jnp.float32)
    for k in range(count):
        mot[1 + each * k: 1 + each * (k + 1)] = mots[k][...]
        mot_edge[8 + 8 * each * k: 8 + 8 * each * (k + 1)] = edges[k][...].reshape(8 * each, hid)
    block = 32

    pieces = []
    for a in range(3):
        for b in range(3):
            pieces += [
                jnp.concatenate([src[pl.ds(8 * a + 2 * b + side, rows, stride=8), :] for side in range(2)], axis=0)
                .astype(jnp.bfloat16) for src in (hid_edge, mot_edge)]
    weights = jnp.concatenate([gates[t, 0: 2 * hid, hid: 2 * hid] for t in range(9)], axis=0)
    acc = dot(jnp.concatenate(pieces, axis=1), weights) + up_edge[...]
    centre = jnp.concatenate([hid_edge[pl.ds(8 + 2 + side, rows, stride=8), :] for side in range(2)], axis=0)
    reset = jax.nn.sigmoid(acc) * centre
    wide[pl.ds(7, rows, stride=32), :] = reset[:rows]
    wide[pl.ds(24, rows, stride=32), :] = reset[rows:]

    def taps(weights, source, r0):
        pieces = []
        for a in range(3):
            one = source[pl.ds(r0 + a, block)].reshape(block * 16, 3 * hid)
            two = mot[pl.ds(r0 + a, block)].reshape(block * 16, 3 * hid)
            for b in range(3):
                pieces += [one[:, b * hid:(b + 1) * hid], two[:, b * hid:(b + 1) * hid]]
        return dot(jnp.concatenate(pieces, axis=1), jnp.concatenate([weights[t, 0: 2 * hid, :] for t in range(9)], axis=0))

    def upsampled(g, *refs):
        parts = []
        for cell in range(block // 8):
            kinds = [jnp.concatenate([ref[g * (block // 8) + cell, kind] for ref in refs], axis=1) for kind in range(3)]
            parts += [kinds[0]] + [kinds[1]] * 6 + [kinds[2]]
        return jnp.concatenate(parts, axis=0)

    def gate_body(g, carry):
        r0 = g * block
        acc = taps(gates, hid3, r0) + upsampled(g, up_z, up_r)
        both = jax.nn.sigmoid(acc)
        h = state[pl.ds(r0, block)].reshape(block * 16, hid).astype(jnp.float32)
        z_keep[pl.ds(r0 * 16, block * 16), :] = both[:, :hid]
        reset = both[:, hid:] * h
        for k in range(block):
            wide[pl.ds(pl.multiple_of((r0 + k) * 32, 32) + 8, 16), :] = reset[16 * k: 16 * k + 16]
        for k in range(block):
            res3[r0 + k + 1] = jnp.concatenate(
                [wide[pl.ds(pl.multiple_of((r0 + k) * 32, 32) + 7 + b, 16), :].astype(jnp.bfloat16)
                 for b in range(3)], axis=1)
        return carry

    lax.fori_loop(0, rows // block, gate_body, 0)

    def cand_body(g, carry):
        r0 = g * block
        q = jnp.tanh(taps(cand, res3, r0) + upsampled(g, up_q))
        h = state[pl.ds(r0, block)].reshape(block * 16, hid).astype(jnp.float32)
        z = z_keep[pl.ds(r0 * 16, block * 16), :]
        new = (1.0 - z) * h + z * q
        out[pl.ds(r0, block)] = new.astype(jnp.bfloat16).reshape(block, 16, hid)
        return carry

    lax.fori_loop(0, rows // block, cand_body, 0)


def fine_gru(i, before, hid3, state, hid_edge, mots, edges, ups, up_edge, gates, cand):
    images, rows, cols, hid = state.shape
    count = len(mots)
    vmem = pl.BlockSpec(memory_space=pltpu.VMEM)
    tall = rows // 8

    def kernel(hid3, state, hid_edge, *refs):
        refs = list(refs)
        if before is not None:
            refs = refs[1:]
        for n in range(3):
            refs[2 * count + n] = refs[2 * count + n].at[pl.ds(tall * i, tall)]
        refs[2 * count + 3] = refs[2 * count + 3].at[i]
        gru_kernel(count, hid3.at[i], state.at[i], hid_edge.at[i], *refs)

    args = [hid3, state, hid_edge]
    rest = [*mots, *edges, *(u.reshape(-1, 3, 16, hid) for u in ups), up_edge, gates, cand]
    first = [] if before is None else [before]
    return pl.pallas_call(
        kernel,
        grid=(1,),
        out_shape=jax.ShapeDtypeStruct(state.shape, jnp.bfloat16),
        in_specs=[vmem] * 3 + [pl.BlockSpec(memory_space=pl.ANY)] * len(first) + [vmem] * len(rest),
        out_specs=pl.BlockSpec((None, rows, cols, hid), lambda _: (i, 0, 0, 0)),
        input_output_aliases={3: 0} if first else {},
        compiler_params=pltpu.CompilerParams(vmem_limit_bytes=16 << 20),
        scratch_shapes=[pltpu.VMEM((rows + 2, 16, 3 * hid), jnp.bfloat16),
                        pltpu.VMEM((8 * (rows + 2), hid), jnp.float32),
                        pltpu.VMEM((rows * 16, hid), jnp.float32),
                        pltpu.VMEM((rows * 32, hid), jnp.float32),
                        pltpu.VMEM((rows + 2, 16, 3 * hid), jnp.bfloat16)],
        name="fine_gru",
        cost_estimate=cost(5),
    )(*(near(v) for v in args), *first, *(near(v) for v in rest))


def lookup_places():
    level = np.full((2, 128), -1)
    offset = np.zeros((2, 128), np.int64)
    for group, first, k in ((0, 0, 3), (0, 72, 2), (1, 0, 1), (1, 18, 0)):
        count = (2 * RADIUS + 1) << k
        level[group, first: first + count] = k
        offset[group, first: first + count] = ((RADIUS + 1) << k) - 1 - np.arange(count)
    tap = np.where(level >= 0, (offset >> np.maximum(level, 0)) + RADIUS, 0)
    return level, offset, tap


def lookup_pick(channels):
    level, _, tap = (v.reshape(-1) for v in lookup_places())
    rows = np.maximum(level, 0) * (2 * RADIUS + 1) + tap
    pick = np.zeros((level.size, channels), np.float32)
    pick[np.arange(level.size), rows] = np.where(level >= 0, 0.5 ** np.maximum(level, 0), 0.0)
    return jnp.asarray(pick.astype(jnp.bfloat16))


def local(left_feat, right_feat, bounds, disparity, hidden_fine, hidden_coarse, motion_weight,
          fine_gates, fine_candidate, coarse_gates, coarse_candidate):
    images, rows, cols, channels = left_feat.shape
    hid = hidden_fine.shape[-1]
    many = images * rows
    each = rows // CHUNKS
    keys = [(i, k) for i in range(images) for k in range(CHUNKS)]
    bf16, f32 = jnp.bfloat16, jnp.float32

    own = [right_feat[i, k * each:(k + 1) * each] for i, k in keys]

    disp = disparity.reshape(many, cols)
    cells = hidden_coarse.shape[1] * hidden_coarse.shape[2] * images
    to_next, to_prev, to_far, flat = call(
        functools.partial(pack_kernel, len(own)), "pack",
        [((3 * many + cells + 16, channels), bf16), ((5 * many + cells + 16, channels), bf16), ((many, channels), bf16),
         ((cells, channels), bf16)],
        [pltpu.VMEM((cells, hid), f32)],
        (left_feat, *own, hidden_fine, hidden_coarse.reshape(-1, hid), disp), 1)
    prev = permute(to_next, lambda j: j + 1)
    foll = permute(to_prev, lambda j: j - 1)
    far = permute(to_far, lambda j: j + 5)
    behind2 = permute(flat, lambda j: j + 2)
    ahead2 = permute(flat, lambda j: j - 2)
    own, prev, foll, far, behind2, ahead2 = lax.optimization_barrier((own, prev, foll, far, behind2, ahead2))
    b4 = [permute(value, lambda j: j + 4) for value in own]
    chosen, b2, core = [], [], []

    def along_y(n, *others):
        chosen.append(choose(own[n], after(b4[n], *others)))
        b2.append(permute(chosen[n], lambda j: j ^ 2))

    def joined(n, *others):
        both = join(after(b2[n], *others), own[n], b4[n])
        core.append(permute(both, lambda j: j ^ 1))
        return both

    where_x = np.array(list(range(cols)) + list(EDGE), np.int32)[:, None]
    lane = np.arange(128, dtype=np.int32)[None]
    column_of = np.where(lane == 127, -65, np.where(lane < 82, lane - 64, 1000))
    distance = where_x - column_of
    distance = jnp.asarray(np.where((distance >= 0) & (distance < MAXD), distance, -1).astype(np.int32))
    _, offset, _ = lookup_places()
    start = jnp.asarray((where_x + 64 - offset[:, None, :]).astype(np.int32))
    pick = lookup_pick(motion_weight.shape[0])

    left_edge, right_edge, disp24, hid_edge, hid3, table, scale = call(
        edge_kernel, "edges",
        [((images, rows, 8, channels), bf16), ((images, rows, 16, channels), bf16), ((images, rows, 24, 128), jnp.int32),
         ((images, 8 * (rows + 2), hid), f32), ((images, rows + 2, cols, 3 * hid), bf16), ((pick.shape[0], hid), bf16),
         ((images, 24, 128), f32)],
        [pltpu.VMEM((16 * 32, hid), f32)],
        (bounds, prev, foll, far, to_next, to_prev, hidden_fine, disp, pick, motion_weight, distance), 2, smem=1)
    new, *ups, up_edge = call(
        coarse_kernel, "coarse",
        [((cells, hid), bf16)] + [((cells // 2 * 48, hid), f32)] * 3 + [((images, 2 * rows, hid), f32)],
        [pltpu.VMEM((2, 5 * cells, hid), f32), pltpu.VMEM((3, 4 * cells, 2 * hid), bf16), pltpu.VMEM((cells, hid), f32)],
        (behind2, prev, flat, foll, ahead2, coarse_gates, coarse_candidate, fine_gates, fine_candidate), 1.5)
    coarse_new = new.reshape(hidden_coarse.shape)

    motions = []

    def motion(n, *others):
        i, k = keys[n]
        motions.append(motion_chunk(i, k, scale, left_feat, left_edge, own[n], right_edge, b4[n], b2[n],
                                    after(core[n], *others), disp24, start, table))
        return motions[n]

    def fine(i, before, *others):
        mine = [m for m, key in zip(motions, keys) if key[0] == i]
        return fine_gru(i, before, after(hid3, *others), hidden_fine, hid_edge, [m for m, _ in mine], [e for _, e in mine],
                        ups, up_edge, fine_gates, fine_candidate)

    along_y(0, table, new)
    along_y(1)
    along_y(2)
    along_y(3)
    for n in range(4):
        joined(n)
    for n in range(4):
        motion(n)
    result = fine(0, None)
    return (fine(1, result), coarse_new)


def solution(mesh):
    return jax.shard_map(
        local,
        mesh=mesh,
        in_specs=(
            P("groups", None, "cols", None),
            P("groups", None, "cols", None),
            P("groups"),
            P("groups", None, "cols"),
            P("groups", None, "cols", None),
            P("groups", None, "cols", None),
            P(),
            P(),
            P(),
            P(),
            P(),
        ),
        out_specs=(P("groups", None, "cols", None), P("groups", None, "cols", None)),
        check_vma=False,
    )
```

```python
import functools

import jax
import jax.numpy as jnp
import numpy as np
from jax import lax
from jax.experimental import pallas as pl
from jax.experimental.pallas import tpu as pltpu
from jax.sharding import PartitionSpec as P

LEVELS = 4
RADIUS = 4
MAXD = 64
CHUNKS = 2
EDGE = (-2, 15, -1, 16, 0, 17, 0, 0)


def permute(value, target, take=lambda j: True):
    count = lax.axis_size("cols")
    pairs = [(j, target(j) % count) for j in range(count) if take(j)]
    return lax.ppermute(value, "cols", pairs)


def near(value):
    return pltpu.with_memory_space_constraint(value, pltpu.VMEM)


def dot(a, b):
    return jnp.dot(a, b, preferred_element_type=jnp.float32)


def onehot(shape, column):
    r = lax.broadcasted_iota(jnp.int32, shape, 0)
    c = lax.broadcasted_iota(jnp.int32, shape, 1)
    return jnp.where(column(r, c), 1.0, 0.0).astype(jnp.bfloat16)


def cost(us):
    return pl.CostEstimate(flops=0, bytes_accessed=int(us * 3.5e6), transcendentals=0)


def call(kernel, name, outs, scratch, args, us, limit=8, smem=0, **kw):
    vmem = pl.BlockSpec(memory_space=pltpu.VMEM)
    return pl.pallas_call(
        kernel,
        out_shape=tuple(pltpu.VMEM(shape, dtype) for shape, dtype in outs),
        in_specs=[pl.BlockSpec(memory_space=pltpu.SMEM)] * smem + [vmem] * (len(args) - smem),
        out_specs=(vmem,) * len(outs),
        scratch_shapes=scratch,
        compiler_params=pltpu.CompilerParams(vmem_limit_bytes=limit << 20),
        name=name,
        cost_estimate=cost(us),
        **kw,
    )(*args[:smem], *(near(a) for a in args[smem:]))


def pack_kernel(count, left, *refs):
    rights = refs[:count]
    state, coarse, disp, to_next, to_prev, far, flat, pooled = refs[count:]
    images, rows, cols, channels = left.shape
    hid = state.shape[-1]
    many = images * rows
    wide = 16 * cols
    each = many // count

    def end(q):
        return q + jnp.where(q >= 2, cols - 4, 0)

    ends = onehot((64, wide), lambda r, c: c == (r & 15) * cols + end(r >> 4))
    per_cell = onehot((8, wide), lambda r, c: (r == (c // (8 * cols)) * (cols // 8) + (c % cols) // 8))
    for b in range(many // 16):
        i, r0 = divmod(16 * b, rows)
        here = pl.ds(16 * b, 16)

        def put(ref, slot, value):
            ref[pl.ds(many * slot + 16 * b, 16), :] = value.astype(jnp.bfloat16)

        e = dot(ends, left[i, r0: r0 + 16].reshape(wide, channels))
        put(to_prev, 0, e[:16])
        put(to_prev, 1, e[16:32])
        put(to_next, 0, e[32:48])
        put(to_next, 1, e[48:])
        e = dot(ends, rights[16 * b // each][16 * b % each: 16 * b % each + 16].reshape(wide, channels))
        put(to_prev, 2, e[:16])
        put(to_prev, 3, e[16:32])
        put(far, 0, e[48:])
        fine = state[i, r0: r0 + 16].reshape(wide, hid)
        e = dot(ends, fine)
        put(to_prev, 4, jnp.concatenate([e[:16], e[16:32]], axis=1))
        put(to_next, 2, jnp.concatenate([e[32:48], e[48:]], axis=1))
        cells = 2 * (cols // 8)
        pooled[pl.ds(cells * b, cells), :] = (dot(per_cell, fine) * (1.0 / 64))[:cells]
    both = jnp.concatenate([coarse[...], pooled[...].astype(jnp.bfloat16)], axis=1)
    flat[...] = both
    to_next[pl.ds(3 * many, flat.shape[0]), :] = both
    to_prev[pl.ds(5 * many, flat.shape[0]), :] = both
    pick = onehot((16, cols), lambda r, c: (c == end(r)) & (r < 4))
    d = lax.dot_general(pick, disp[...].astype(jnp.float32).astype(jnp.bfloat16), (((1,), (1,)), ((), ())),
                        preferred_element_type=jnp.float32)
    d = jnp.concatenate([d, jnp.zeros((16, channels - many), jnp.float32)], axis=1).astype(jnp.bfloat16)
    to_next[pl.ds(3 * many + flat.shape[0], 16), :] = d
    to_prev[pl.ds(5 * many + flat.shape[0], 16), :] = d


def edge_kernel(bounds, prev, foll, far, to_next, to_prev, state, disp, pick, motion_weight, distance, left_edge, right_edge, disp24, hid_edge,
                hid3, table, scale, wide):
    table[...] = dot(pick[...], motion_weight[...]).astype(jnp.bfloat16)
    images, rows, cols, hid = state.shape
    many = images * rows
    channels = prev.shape[1]
    for i in range(images):
        known = (distance[...] >= 0) & (distance[...] < bounds[i])
        scale[i] = jnp.where(known, jnp.float32(channels ** -0.5), 0.0)
    last = prev.shape[0] - 16
    spread8 = onehot((128, 96), lambda r, c: c == (r & 7) * 16 + (r >> 3))
    spread16 = onehot((256, 48), lambda r, c: c == jnp.where((r & 15) == 15, 2, jnp.where((r & 15) < 2, r & 15, 9)) * 16 + (r >> 4))

    own = disp[...].astype(jnp.float32).astype(jnp.bfloat16)
    d24 = dot(own, onehot((cols, cols + 8), lambda r, c: (r == c) | ((c == cols + 1) & (r == cols - 1))
                          | ((c == cols + 4) & (r == 0))))
    for ref, first, slots in ((prev, last, ((2, 0), (3, 2))), (foll, foll.shape[0] - 16, ((0, 3), (1, 5)))):
        rows16 = ref[pl.ds(first, 16), :many]
        place = onehot((16, cols + 8), lambda r, c: ((r == slots[0][0]) & (c == cols + slots[0][1]))
                       | ((r == slots[1][0]) & (c == cols + slots[1][1])))
        d24 += lax.dot_general(rows16, place, (((0,), (0,)), ((), ())), preferred_element_type=jnp.float32)
    d24 = d24.astype(jnp.bfloat16)
    slots = cols + 8
    repeat = onehot((16 * slots, 16), lambda r, c: c == r // slots)
    match = lax.broadcasted_iota(jnp.int32, (16 * slots, slots), 0) % slots \
        == lax.broadcasted_iota(jnp.int32, (16 * slots, slots), 1)
    ones = jnp.ones((slots, 128), jnp.bfloat16)

    for i in range(images):
        for line in (0, rows + 1):
            hid3[i, line] = jnp.zeros((cols, 3 * hid), jnp.bfloat16)
            hid_edge[i, pl.ds(8 * line, 8), :] = jnp.zeros((8, hid), jnp.float32)
    for b in range(many // 16):
        i, r0 = divmod(16 * b, rows)

        def get(ref, slot):
            return ref[pl.ds(many * slot + 16 * b, 16), :]

        e = dot(spread8, jnp.concatenate([get(prev, 0), get(to_next, 1), get(prev, 1), get(foll, 0), get(to_prev, 0),
                                          get(foll, 1)], axis=0))
        left_edge[i, r0: r0 + 16] = e.reshape(16, 8, channels).astype(jnp.bfloat16)
        e = dot(spread16, jnp.concatenate([get(foll, 2), get(foll, 3), get(far, 0)], axis=0))
        right_edge[i, r0: r0 + 16] = e.reshape(16, 16, channels).astype(jnp.bfloat16)
        hp, hn, on, op = get(prev, 2), get(foll, 4), get(to_next, 2), get(to_prev, 4)
        e = dot(spread8, jnp.concatenate([hp[:, :hid], on[:, hid:], hp[:, hid:], hn[:, :hid], op[:, :hid], hn[:, hid:]],
                                         axis=0))
        hid_edge[i, pl.ds(8 + 8 * r0, 128), :] = e
        for k in range(16):
            wide[pl.ds(32 * k + 8, cols), :] = state[i, r0 + k].astype(jnp.float32)
        wide[pl.ds(7, 16, stride=32), :] = hp[:, hid:].astype(jnp.float32)
        wide[pl.ds(8 + cols, 16, stride=32), :] = hn[:, :hid].astype(jnp.float32)
        for k in range(16):
            hid3[i, 1 + r0 + k] = jnp.concatenate(
                [wide[pl.ds(32 * k + 7 + t, cols), :].astype(jnp.bfloat16) for t in range(3)], axis=1)
        spread = jnp.where(match, dot(repeat, d24[16 * b: 16 * b + 16]), 0.0).astype(jnp.bfloat16)
        disp24[i, r0: r0 + 16] = dot(spread, ones).astype(jnp.int32).reshape(16, slots, 128)


def coarse_kernel(behind2, prev, flat, foll, ahead2, gates, cand, fine_gates, fine_cand, new, up_z, up_r, up_q, up_edge,
                  columns, shifted, scratch):
    count = flat.shape[0]
    cells = count // 2
    hid = new.shape[1]
    images = up_edge.shape[0]
    tall = cells // images

    def moved(value, by):
        row = lax.broadcasted_iota(jnp.int32, value.shape, 0) % tall
        if by > 0:
            return jnp.where(row == 0, 0.0, pltpu.roll(value, 1, 0))
        return jnp.where(row == tall - 1, 0.0, pltpu.roll(value, value.shape[0] - 1, 0))

    many3, many5 = prev.shape[0] - 16 - count, foll.shape[0] - 16 - count
    sources = (behind2[...], prev[pl.ds(many3, count), :], flat[...], foll[pl.ds(many5, count), :], ahead2[...])
    for n, source in enumerate(sources):
        for half in range(2):
            columns[half, pl.ds(count * n, count), :] = source[:, half * hid:(half + 1) * hid].astype(jnp.float32)
    state = []
    for n in range(8):
        parts = [columns[half, pl.ds(count * ((n + 1) // 2) + (n + 1) % 2, cells, stride=2), :] for half in range(2)]
        state.append(parts[0])
        both = jnp.concatenate(parts, axis=1)
        for a in range(3):
            value = both if a == 1 else moved(both, 1 - a)
            shifted[a, pl.ds(cells * n, cells), :] = value.astype(jnp.bfloat16)
    acc = jnp.zeros((6 * cells, 2 * hid), jnp.float32)
    for a in range(3):
        for b in range(3):
            acc += dot(shifted[a, pl.ds(cells * b, 6 * cells), :], gates[3 * a + b])
    zr = jax.nn.sigmoid(acc)
    reset = zr[:, hid:] * jnp.concatenate(state[1:7], axis=0)
    reset = reset.astype(jnp.bfloat16).astype(jnp.float32)
    acc = jnp.zeros((4 * cells, hid), jnp.float32)
    for a in range(3):
        value = (reset if a == 1 else moved(reset, 1 - a)).astype(jnp.bfloat16)
        for b in range(3):
            lhs = jnp.concatenate([value[cells * b: cells * (b + 4)],
                                   shifted[a, pl.ds(cells * (b + 1), 4 * cells), hid:]], axis=1)
            acc += dot(lhs, cand[3 * a + b])
    q = jnp.tanh(acc)
    z = zr[cells: 5 * cells, :hid]
    fresh = (1.0 - z) * jnp.concatenate(state[2:6], axis=0) + z * q
    rounded = fresh.astype(jnp.bfloat16)
    for n in range(2):
        scratch[pl.ds(n, cells, stride=2), :] = fresh[cells * (n + 1): cells * (n + 2)]
    new[...] = scratch[...].astype(jnp.bfloat16)

    sums = []
    for b in range(3):
        p = []
        for a in range(3):
            w = jnp.concatenate([fine_gates[3 * a + b, 2 * hid:, :], fine_cand[3 * a + b, 2 * hid:, :]], axis=1)
            p.append(dot(rounded, w))
        low = p[0] + p[1]
        sums.append((moved(p[0], 1) + p[1] + p[2], low + p[2], low + moved(p[2], -1)))

    def at(kind, js):
        return sum(sums[b][kind][cells * (js[b] + 1): cells * (js[b] + 2)] for b in range(3))

    for kind in range(3):
        inner = {0: (-1, 0, 0), 7: (0, 0, 1), 8: (0, 1, 1), 15: (1, 1, 2)}
        flat0, flat1 = at(kind, (0, 0, 0)), at(kind, (1, 1, 1))
        for x in range(16):
            value = at(kind, inner[x]) if x in inner else (flat0 if x < 8 else flat1)
            for part, ref in enumerate((up_z, up_r, up_q)):
                ref[pl.ds(kind * 16 + x, cells, stride=48), :] = value[:, part * hid:(part + 1) * hid]
        for side, js in enumerate(((-1, -1, 0), (1, 2, 2))):
            value = at(kind, js)[:, hid: 2 * hid]
            for i in range(images):
                for u in ((0,), range(1, 7), (7,))[kind]:
                    up_edge[i, pl.ds(side * 8 * tall + u, tall, stride=8), :] = value[tall * i: tall * (i + 1)]


def copy_either(second_wanted, first, second, out):
    @pl.when(jnp.logical_not(second_wanted))
    def _():
        out[...] = first[...]

    @pl.when(second_wanted)
    def _():
        out[...] = second[...]


def choose_kernel(mine, came, out):
    copy_either(lax.rem(lax.axis_index("cols"), 4) >= 2, mine, came, out)


def choose(mine, came):
    return call(choose_kernel, "choose", [(mine.shape, mine.dtype)], [], (mine, came), 0.2)[0]


def join_kernel(second, mine, came, out):
    out[0] = second[...]
    copy_either(lax.rem(lax.axis_index("cols"), 2) == 1, mine, came, out.at[1])


def join(second, mine, came):
    return call(join_kernel, "join", [((2,) + mine.shape, mine.dtype)], [], (second, mine, came), 0.3)[0]


def after(values, *others):
    return lax.optimization_barrier((values, others))[0]


def corr_kernel(scale, left, left_edge, right, right_edge, b4, b2, core, disp, start, table,
                mot3, mot_edge, wide):
    rows = right.shape[0]
    group = 32
    odd = lax.rem(lax.axis_index("cols"), 2)
    scale = scale[...]
    lane = lax.broadcasted_iota(jnp.int32, (24, 128), 1)
    keep = (jnp.where(lane < 72, ~7, ~3), jnp.where(lane < 18, ~1, ~0))
    last_lane = lax.broadcasted_iota(jnp.int32, (8, 128), 1) == 127

    def body(g, carry):
        scores, places = [], ([], [])
        for k in range(group):
            h = g * group + k
            window = jnp.concatenate(
                [b4[h], core[1 - odd, h], b2[h], core[odd, h], right[h], right_edge[h]], axis=0)
            pixels = jnp.concatenate([left[h], left_edge[h]], axis=0)
            s = lax.dot_general(pixels, window, (((1,), (1,)), ((), ())), preferred_element_type=jnp.float32)
            s = jnp.concatenate([s, jnp.zeros((s.shape[0], 128 - s.shape[1]), jnp.float32)], axis=1)
            ends = jnp.where(last_lane, pltpu.roll(s[16:], 32, 1), s[16:])
            scores.append(s[:16] * scale[:16])
            scores.append(ends * scale[16:])
            d = disp[h]
            for n in range(2):
                places[n].append((start[n] - (d & keep[n])) & 127)
        c = jnp.concatenate(scores, axis=0)
        found = [jnp.take_along_axis(c, jnp.concatenate(p, axis=0), axis=1, mode="promise_in_bounds") for p in places]
        motion = jnp.maximum(dot(jnp.concatenate(found, axis=1).astype(jnp.bfloat16), table[...]), 0.0)
        for k in range(group):
            h = g * group + k
            m = motion[24 * k: 24 * k + 24]
            wide[pl.ds(32 * k + 8, 16), :] = m[:16]
            mot_edge[h] = m[16:]
            wide[pl.ds(32 * k + 7, 1), :] = m[18:19]
            wide[pl.ds(32 * k + 24, 1), :] = m[19:20]
        for k in range(group):
            h = g * group + k
            mot3[h] = jnp.concatenate(
                [wide[pl.ds(32 * k + 7 + b, 16), :].astype(jnp.bfloat16) for b in range(3)], axis=1)
        return carry

    lax.fori_loop(0, rows // group, body, 0)


def motion_chunk(i, k, scale, left, left_edge, right, right_edge, b4, b2, core, disp, start, table):
    rows = b4.shape[0]
    hid = table.shape[1]

    def kernel(scale, left, left_edge, right, right_edge, b4, b2, core, disp, *rest):
        here = pl.ds(k * rows, rows)
        corr_kernel(scale.at[i], left.at[i, here], left_edge.at[i, here], right, right_edge.at[i, here],
                    b4, b2, core, disp.at[i, here], *rest)

    return call(kernel, "motion", [((rows, 16, 3 * hid), jnp.bfloat16), ((rows, 8, hid), jnp.float32)],
                [pltpu.VMEM((32 * 32, hid), jnp.float32)],
                (scale, left, left_edge, right, right_edge, b4, b2, core, disp, start, table), 2.7)


def gru_kernel(count, hid3, state, hid_edge, *refs):
    mots, edges = refs[:count], refs[count:2 * count]
    (up_z, up_r, up_q, up_edge, gates, cand, out, mot, mot_edge, z_keep, wide, res3) = refs[2 * count:]
    rows = state.shape[0]
    hid = state.shape[-1]
    each = rows // count
    zero = jnp.zeros((1, 16, 3 * hid), jnp.bfloat16)
    mot[0:1] = zero
    mot[rows + 1: rows + 2] = zero
    res3[0:1] = zero
    res3[rows + 1: rows + 2] = zero
    mot_edge[0:8] = jnp.zeros((8, hid), jnp.float32)
    mot_edge[8 * (rows + 1): 8 * (rows + 2)] = jnp.zeros((8, hid), jnp.float32)
    for k in range(count):
        mot[1 + each * k: 1 + each * (k + 1)] = mots[k][...]
        mot_edge[8 + 8 * each * k: 8 + 8 * each * (k + 1)] = edges[k][...].reshape(8 * each, hid)
    block = 32

    pieces = []
    for a in range(3):
        for b in range(3):
            pieces += [
                jnp.concatenate([src[pl.ds(8 * a + 2 * b + side, rows, stride=8), :] for side in range(2)], axis=0)
                .astype(jnp.bfloat16) for src in (hid_edge, mot_edge)]
    weights = jnp.concatenate([gates[t, 0: 2 * hid, hid: 2 * hid] for t in range(9)], axis=0)
    acc = dot(jnp.concatenate(pieces, axis=1), weights) + up_edge[...]
    centre = jnp.concatenate([hid_edge[pl.ds(8 + 2 + side, rows, stride=8), :] for side in range(2)], axis=0)
    reset = jax.nn.sigmoid(acc) * centre
    wide[pl.ds(7, rows, stride=32), :] = reset[:rows]
    wide[pl.ds(24, rows, stride=32), :] = reset[rows:]

    def taps(weights, source, r0):
        pieces = []
        for a in range(3):
            one = source[pl.ds(r0 + a, block)].reshape(block * 16, 3 * hid)
            two = mot[pl.ds(r0 + a, block)].reshape(block * 16, 3 * hid)
            for b in range(3):
                pieces += [one[:, b * hid:(b + 1) * hid], two[:, b * hid:(b + 1) * hid]]
        return dot(jnp.concatenate(pieces, axis=1), jnp.concatenate([weights[t, 0: 2 * hid, :] for t in range(9)], axis=0))

    def upsampled(g, *refs):
        parts = []
        for cell in range(block // 8):
            kinds = [jnp.concatenate([ref[g * (block // 8) + cell, kind] for ref in refs], axis=1) for kind in range(3)]
            parts += [kinds[0]] + [kinds[1]] * 6 + [kinds[2]]
        return jnp.concatenate(parts, axis=0)

    def gate_body(g, carry):
        r0 = g * block
        acc = taps(gates, hid3, r0) + upsampled(g, up_z, up_r)
        both = jax.nn.sigmoid(acc)
        h = state[pl.ds(r0, block)].reshape(block * 16, hid).astype(jnp.float32)
        z_keep[pl.ds(r0 * 16, block * 16), :] = both[:, :hid]
        reset = both[:, hid:] * h
        for k in range(block):
            wide[pl.ds(pl.multiple_of((r0 + k) * 32, 32) + 8, 16), :] = reset[16 * k: 16 * k + 16]
        for k in range(block):
            res3[r0 + k + 1] = jnp.concatenate(
                [wide[pl.ds(pl.multiple_of((r0 + k) * 32, 32) + 7 + b, 16), :].astype(jnp.bfloat16)
                 for b in range(3)], axis=1)
        return carry

    lax.fori_loop(0, rows // block, gate_body, 0)

    block = 64

    def cand_body(g, carry):
        r0 = g * block
        q = jnp.tanh(taps(cand, res3, r0) + upsampled(g, up_q))
        h = state[pl.ds(r0, block)].reshape(block * 16, hid).astype(jnp.float32)
        z = z_keep[pl.ds(r0 * 16, block * 16), :]
        new = (1.0 - z) * h + z * q
        out[pl.ds(r0, block)] = new.astype(jnp.bfloat16).reshape(block, 16, hid)
        return carry

    lax.fori_loop(0, rows // block, cand_body, 0)


def fine_gru(i, before, hid3, state, hid_edge, mots, edges, ups, up_edge, gates, cand):
    images, rows, cols, hid = state.shape
    count = len(mots)
    vmem = pl.BlockSpec(memory_space=pltpu.VMEM)
    tall = rows // 8

    def kernel(hid3, state, hid_edge, *refs):
        refs = list(refs)
        if before is not None:
            refs = refs[1:]
        for n in range(3):
            refs[2 * count + n] = refs[2 * count + n].at[pl.ds(tall * i, tall)]
        refs[2 * count + 3] = refs[2 * count + 3].at[i]
        gru_kernel(count, hid3.at[i], state.at[i], hid_edge.at[i], *refs)

    args = [hid3, state, hid_edge]
    rest = [*mots, *edges, *(u.reshape(-1, 3, 16, hid) for u in ups), up_edge, gates, cand]
    first = [] if before is None else [before]
    return pl.pallas_call(
        kernel,
        grid=(1,),
        out_shape=jax.ShapeDtypeStruct(state.shape, jnp.bfloat16),
        in_specs=[vmem] * 3 + [pl.BlockSpec(memory_space=pl.ANY)] * len(first) + [vmem] * len(rest),
        out_specs=pl.BlockSpec((None, rows, cols, hid), lambda _: (i, 0, 0, 0)),
        input_output_aliases={3: 0} if first else {},
        compiler_params=pltpu.CompilerParams(vmem_limit_bytes=16 << 20),
        scratch_shapes=[pltpu.VMEM((rows + 2, 16, 3 * hid), jnp.bfloat16),
                        pltpu.VMEM((8 * (rows + 2), hid), jnp.float32),
                        pltpu.VMEM((rows * 16, hid), jnp.float32),
                        pltpu.VMEM((rows * 32, hid), jnp.float32),
                        pltpu.VMEM((rows + 2, 16, 3 * hid), jnp.bfloat16)],
        name="fine_gru",
        cost_estimate=cost(5),
    )(*(near(v) for v in args), *first, *(near(v) for v in rest))


def lookup_places():
    level = np.full((2, 128), -1)
    offset = np.zeros((2, 128), np.int64)
    for group, first, k in ((0, 0, 3), (0, 72, 2), (1, 0, 1), (1, 18, 0)):
        count = (2 * RADIUS + 1) << k
        level[group, first: first + count] = k
        offset[group, first: first + count] = ((RADIUS + 1) << k) - 1 - np.arange(count)
    tap = np.where(level >= 0, (offset >> np.maximum(level, 0)) + RADIUS, 0)
    return level, offset, tap


def lookup_pick(channels):
    level, _, tap = (v.reshape(-1) for v in lookup_places())
    rows = np.maximum(level, 0) * (2 * RADIUS + 1) + tap
    pick = np.zeros((level.size, channels), np.float32)
    pick[np.arange(level.size), rows] = np.where(level >= 0, 0.5 ** np.maximum(level, 0), 0.0)
    return jnp.asarray(pick.astype(jnp.bfloat16))


def local(left_feat, right_feat, bounds, disparity, hidden_fine, hidden_coarse, motion_weight,
          fine_gates, fine_candidate, coarse_gates, coarse_candidate):
    images, rows, cols, channels = left_feat.shape
    hid = hidden_fine.shape[-1]
    many = images * rows
    each = rows // CHUNKS
    keys = [(i, k) for i in range(images) for k in range(CHUNKS)]
    bf16, f32 = jnp.bfloat16, jnp.float32

    own = [right_feat[i, k * each:(k + 1) * each] for i, k in keys]

    disp = disparity.reshape(many, cols)
    cells = hidden_coarse.shape[1] * hidden_coarse.shape[2] * images
    to_next, to_prev, to_far, flat = call(
        functools.partial(pack_kernel, len(own)), "pack",
        [((3 * many + cells + 16, channels), bf16), ((5 * many + cells + 16, channels), bf16), ((many, channels), bf16),
         ((cells, channels), bf16)],
        [pltpu.VMEM((cells, hid), f32)],
        (left_feat, *own, hidden_fine, hidden_coarse.reshape(-1, hid), disp), 1)
    prev = permute(to_next, lambda j: j + 1)
    foll = permute(to_prev, lambda j: j - 1)
    far = permute(to_far, lambda j: j + 5)
    behind2 = permute(flat, lambda j: j + 2)
    ahead2 = permute(flat, lambda j: j - 2)
    own, prev, foll, far, behind2, ahead2 = lax.optimization_barrier((own, prev, foll, far, behind2, ahead2))
    b4 = [permute(value, lambda j: j + 4) for value in own]
    chosen, b2, core = [], [], []

    def along_y(n, *others):
        chosen.append(choose(own[n], after(b4[n], *others)))
        b2.append(permute(chosen[n], lambda j: j ^ 2))

    def joined(n, *others):
        both = join(after(b2[n], *others), own[n], b4[n])
        core.append(permute(both, lambda j: j ^ 1))
        return both

    where_x = np.array(list(range(cols)) + list(EDGE), np.int32)[:, None]
    lane = np.arange(128, dtype=np.int32)[None]
    column_of = np.where(lane == 127, -65, np.where(lane < 82, lane - 64, 1000))
    distance = where_x - column_of
    distance = jnp.asarray(np.where((distance >= 0) & (distance < MAXD), distance, -1).astype(np.int32))
    _, offset, _ = lookup_places()
    start = jnp.asarray((where_x + 64 - offset[:, None, :]).astype(np.int32))
    pick = lookup_pick(motion_weight.shape[0])

    left_edge, right_edge, disp24, hid_edge, hid3, table, scale = call(
        edge_kernel, "edges",
        [((images, rows, 8, channels), bf16), ((images, rows, 16, channels), bf16), ((images, rows, 24, 128), jnp.int32),
         ((images, 8 * (rows + 2), hid), f32), ((images, rows + 2, cols, 3 * hid), bf16), ((pick.shape[0], hid), bf16),
         ((images, 24, 128), f32)],
        [pltpu.VMEM((16 * 32, hid), f32)],
        (bounds, prev, foll, far, to_next, to_prev, hidden_fine, disp, pick, motion_weight, distance), 2, smem=1)
    new, *ups, up_edge = call(
        coarse_kernel, "coarse",
        [((cells, hid), bf16)] + [((cells // 2 * 48, hid), f32)] * 3 + [((images, 2 * rows, hid), f32)],
        [pltpu.VMEM((2, 5 * cells, hid), f32), pltpu.VMEM((3, 4 * cells, 2 * hid), bf16), pltpu.VMEM((cells, hid), f32)],
        (behind2, prev, flat, foll, ahead2, coarse_gates, coarse_candidate, fine_gates, fine_candidate), 1.5)
    coarse_new = new.reshape(hidden_coarse.shape)

    motions = []

    def motion(n, *others):
        i, k = keys[n]
        motions.append(motion_chunk(i, k, scale, left_feat, left_edge, own[n], right_edge, b4[n], b2[n],
                                    after(core[n], *others), disp24, start, table))
        return motions[n]

    def fine(i, before, *others):
        mine = [m for m, key in zip(motions, keys) if key[0] == i]
        return fine_gru(i, before, after(hid3, *others), hidden_fine, hid_edge, [m for m, _ in mine], [e for _, e in mine],
                        ups, up_edge, fine_gates, fine_candidate)

    along_y(0, table, new)
    along_y(1)
    along_y(2)
    along_y(3)
    for n in range(4):
        joined(n)
    for n in range(4):
        motion(n)
    result = fine(0, None)
    return (fine(1, result), coarse_new)


def solution(mesh):
    return jax.shard_map(
        local,
        mesh=mesh,
        in_specs=(
            P("groups", None, "cols", None),
            P("groups", None, "cols", None),
            P("groups"),
            P("groups", None, "cols"),
            P("groups", None, "cols", None),
            P("groups", None, "cols", None),
            P(),
            P(),
            P(),
            P(),
            P(),
        ),
        out_specs=(P("groups", None, "cols", None), P("groups", None, "cols", None)),
        check_vma=False,
    )
```
